512 devices in a mesh: segment: 4 (over x), row: 8 (over z), col: 16 (over y, core).
Axes of the slice: x: 4, y: 8, z: 8, core: 2. Of those that a mesh axis runs over, the one named last changes fastest.
Arguments:
- saved_inputs: bfloat16 [4, 1, 128, 256, 256], P('segment', None, 'row', 'col'), may hold values from -6 to 6
- out_grad: bfloat16 [1, 128, 256, 256], P(None, 'row', 'col'), may hold values from -6 to 6
- tissue: int32 [1, 8, 16], P(None, 'row', 'col'), may hold values 0 or 1
- conv_taps: float32 [4, 7, 7, 256], P('segment'), may hold values from -0.875 to 0.875
- conv_bias: float32 [4, 256], P('segment'), may hold values from -3 to 3
- norm_gain: float32 [4, 256], P('segment'), may hold values from 0.1 to 1.9
- norm_bias: float32 [4, 256], P('segment'), may hold values from -3 to 3
- w_in: bfloat16 [4, 256, 1024], P('segment'), may hold values from -0.375 to 0.375
- b_in: float32 [4, 1024], P('segment'), may hold values from -3 to 3
- w_out: bfloat16 [4, 1024, 256], P('segment'), may hold values from -0.1875 to 0.1875
- layer_scale: float32 [4, 256], P('segment'), may hold values from 0.3 to 1.5
Outputs:
- section_grads: bfloat16 [4, 1, 128, 256, 256], P('segment', None, 'row', 'col')
- grad_w_in: float32 [4, 256, 1024], P('segment', 'col')
- grad_w_out: float32 [4, 1024, 256], P('segment', 'col')
- grad_taps: float32 [4, 7, 7, 256], P('segment')
The draws below stay inside these ranges and needn't reach their ends.
Inputs may be any that keep to these rules, and one draw needn't show every extreme that they name: 1 marks a tile that holds tissue, 0 an empty one.
All inputs are finite; a program needn't handle non-finite values. No bound on the sum of `tissue` on one device may be relied on, other than what follows from the above.
Results may differ from the reference program's by a relative error of at most 0.013.
Values may be sent and summed in bfloat16 or wider, within the bound.
A program may use at most 128 MiB of HBM per device.

```python
import math
import jax
import jax.numpy as jnp
from jax import lax

C = 256
HID = 1024
KSIZE = 7
TILE = 16
CROPS = 1
SECTIONS = 4
GR = 8
GC = 16
NH = 128
NW = 256


def place_ends(result, rng, least, top_value):
    place = [jax.random.randint(jax.random.fold_in(rng, axis), (), 0, length) for axis, length in enumerate(result.shape)]
    longest = result.shape.index(max(result.shape))
    beside = place[:longest] + [(place[longest] + 1) % result.shape[longest]] + place[longest + 1:]
    return result.at[tuple(place)].set(least).at[tuple(beside)].set(top_value)


def block_scale(stream_key, dims, cuts, smallest, largest):
    factor_of, own = 1.0, jax.random.fold_in(stream_key, 6)
    for axis_at, parts in cuts:
        heights = jnp.exp(jax.random.uniform(jax.random.fold_in(own, axis_at), (parts,), jnp.float32, smallest / len(cuts), largest / len(cuts)))
        factor_of = factor_of * jnp.repeat(heights, dims[axis_at] // parts).reshape([-1 if axis == axis_at else 1 for axis in range(len(dims))])
    return factor_of


def bell_draw(own_key, extent, scale, most, shards=(), dtype=jnp.bfloat16):
    array = jax.random.normal(own_key, extent, jnp.float32) * scale
    if len(shards) > 0:
        array = block_scale(own_key, extent, shards, -0.22, 0.18) * array
    return jnp.clip(array, min=-most, max=most).astype(dtype)


def setup_inputs(seed: int = 0) -> dict:
    streams_of = jax.random.split(jax.random.key(seed), 12)
    return {
        "saved_inputs": bell_draw(streams_of[0], (SECTIONS, CROPS, NH, NW, C), 1.0, 6.0, ((0, 4), (2, 8), (3, 16))),
        "out_grad": bell_draw(streams_of[1], (CROPS, NH, NW, C), 1.0, 6.0, ((1, 8), (2, 16))),
        "tissue": place_ends((jax.random.randint(streams_of[2], (CROPS, GR, GC), 0, 2) < 1).astype(jnp.int32), jax.random.fold_in(streams_of[2], 1), 0, 1),
        "conv_taps": bell_draw(streams_of[3], (SECTIONS, KSIZE, KSIZE, C), (KSIZE * KSIZE) ** -0.5, 0.875, ((0, 4),), jnp.float32),
        "conv_bias": bell_draw(streams_of[4], (SECTIONS, C), 0.5, 3.0, ((0, 4),), jnp.float32),
        "norm_gain": jnp.clip(1.0 + 0.18 * jax.random.normal(streams_of[5], (SECTIONS, C), jnp.float32), 0.1, 1.9),
        "norm_bias": bell_draw(streams_of[6], (SECTIONS, C), 0.5, 3.0, ((0, 4),), jnp.float32),
        "w_in": bell_draw(streams_of[7], (SECTIONS, C, HID), C ** -0.5, 0.375, ((0, 4),)),
        "b_in": bell_draw(streams_of[8], (SECTIONS, HID), 0.5, 3.0, ((0, 4),), jnp.float32),
        "w_out": bell_draw(streams_of[9], (SECTIONS, HID, C), HID ** -0.5, 0.1875, ((0, 4),)),
        "layer_scale": jnp.clip(jnp.exp(math.log(1.5) - 1.60943787 * jax.random.uniform(streams_of[10], (SECTIONS, C), jnp.float32) ** block_scale(streams_of[10], (SECTIONS, C), ((0, 4),), -0.2, 0.2)), 0.3, 1.5),
    }


epsilon = 1e-06

def depthwise(padded, conv_taps, height, across):
    side = conv_taps.shape[0]
    total = jnp.zeros((height, across, padded.shape[-1]), jnp.float32)
    for shift_r in range(side):
        for shift_c in range(side):
            total = total + conv_taps[shift_r, shift_c] * padded[shift_r:shift_r + height, shift_c:shift_c + across].astype(jnp.float32)
    return total

def transposed(padded_grad, conv_taps, height, across):
    side = conv_taps.shape[0]
    margin = side // 2
    total = jnp.zeros((height, across, padded_grad.shape[-1]), jnp.float32)
    for shift_r in range(side):
        for shift_c in range(side):
            start_r = 2 * margin - shift_r
            start_c = 2 * margin - shift_c
            total = total + conv_taps[shift_r, shift_c] * padded_grad[start_r:start_r + height, start_c:start_c + across].astype(jnp.float32)
    return total

def kernel_grad(padded, grad, height, across):
    side = KSIZE
    grad_wide = grad.astype(jnp.float32)
    pieces = []
    for shift_r in range(side):
        for shift_c in range(side):
            window = padded[shift_r:shift_r + height, shift_c:shift_c + across].astype(jnp.float32)
            pieces.append(lax.optimization_barrier(jnp.sum(window * grad_wide, axis=(0, 1))))
    return jnp.stack(pieces).reshape(side, side, -1)

def pixel_grad(conv_out, upstream, gate, norm_gain, norm_bias, w_in, b_in, w_out, layer_scale):
    average = lax.optimization_barrier(jnp.mean(conv_out, axis=-1, keepdims=True))
    centred = conv_out - average
    spread = lax.optimization_barrier(jnp.mean(centred * centred, axis=-1, keepdims=True))
    inv_std = lax.rsqrt(spread + epsilon)
    standard = centred * inv_std
    normed = (standard * norm_gain + norm_bias).astype(jnp.bfloat16)
    pre_gate = jnp.dot(normed, w_in, preferred_element_type=jnp.float32) + b_in
    gated, gelu_back = jax.vjp(jax.nn.gelu, pre_gate)
    hidden = gated.astype(jnp.bfloat16)
    branch_grad = (gate * layer_scale * upstream.astype(jnp.float32)).astype(jnp.bfloat16)
    grad_out = jnp.dot(hidden.T, branch_grad, preferred_element_type=jnp.float32)
    hidden_grad = jnp.dot(branch_grad, w_out.T, preferred_element_type=jnp.float32)
    pre_grad = gelu_back(hidden_grad)[0].astype(jnp.bfloat16)
    grad_in = jnp.dot(normed.T, pre_grad, preferred_element_type=jnp.float32)
    norm_grad = jnp.dot(pre_grad, w_in.T, preferred_element_type=jnp.float32) * norm_gain
    conv_grad = inv_std * (norm_grad - lax.optimization_barrier(jnp.mean(norm_grad, axis=-1, keepdims=True)) - standard * lax.optimization_barrier(jnp.mean(norm_grad * standard, axis=-1, keepdims=True)))
    return (conv_grad.astype(jnp.bfloat16), grad_in, grad_out)

def reference(saved_inputs, out_grad, tissue, conv_taps, conv_bias, norm_gain, norm_bias, w_in, b_in, w_out, layer_scale):
    margin = KSIZE // 2
    norm_scale = 1.0 / math.sqrt(CROPS * NH * NW)
    upstream_all = out_grad
    section_list = [None] * SECTIONS
    grad_in_list = [None] * SECTIONS
    grad_out_list = [None] * SECTIONS
    grad_taps_list = [None] * SECTIONS
    for section in range(SECTIONS - 1, -1, -1):
        sum_in = jnp.zeros((C, HID), jnp.float32)
        sum_out = jnp.zeros((HID, C), jnp.float32)
        sum_taps = jnp.zeros((KSIZE, KSIZE, C), jnp.float32)
        crop_grads = []
        for crop in range(CROPS):
            saved = saved_inputs[section, crop]
            upstream = upstream_all[crop]
            padded = jnp.pad(saved, ((margin, margin), (margin, margin), (0, 0)))
            conv_out = depthwise(padded, conv_taps[section], NH, NW) + conv_bias[section]
            tile_marks = tissue[crop].astype(jnp.float32)
            pixel_mask = jnp.broadcast_to(tile_marks[:, None, :, None], (GR, TILE, GC, TILE)).reshape(NH, NW)
            conv_grad, grad_in, grad_out = pixel_grad(conv_out.reshape(-1, C), upstream.reshape(-1, C), pixel_mask.reshape(-1, 1), norm_gain[section], norm_bias[section], w_in[section], b_in[section], w_out[section], layer_scale[section])
            conv_grad = conv_grad.reshape(NH, NW, C)
            sum_in = sum_in + grad_in
            sum_out = sum_out + grad_out
            sum_taps = sum_taps + kernel_grad(padded, conv_grad, NH, NW)
            padded_grad = jnp.pad(conv_grad, ((margin, margin), (margin, margin), (0, 0)))
            input_grad = (upstream.astype(jnp.float32) + transposed(padded_grad, conv_taps[section], NH, NW)).astype(jnp.bfloat16)
            crop_grads.append(input_grad)
        upstream_all = jnp.stack(crop_grads)
        section_list[section] = upstream_all
        grad_in_list[section] = sum_in * norm_scale
        grad_out_list[section] = sum_out * norm_scale
        grad_taps_list[section] = sum_taps * norm_scale
    return (jnp.stack(section_list), jnp.stack(grad_in_list), jnp.stack(grad_out_list), jnp.stack(grad_taps_list))
```

```python
import functools
import math

import jax
import jax.numpy as jnp
from jax import lax
from jax.experimental import pallas as pl
from jax.experimental.pallas import tpu as pltpu
from jax.sharding import PartitionSpec as P

F32 = jnp.float32
BF16 = jnp.bfloat16
MESH = pl.DeviceIdType.MESH
EPS = 1e-06
H = 16
W = 16
C = 256
HID = 1024
ROWS = 8
COLS = 16
YS = 8
SEGS = 4
LEFT = 8
PADW = 32
CONV_ROWS = 4
CHUNKS = 2
CH_ROWS = H // CHUNKS
CH_PIX = CH_ROWS * W
DIRS = ((-1, 0), (1, 0), (0, -1), (0, 1), (-1, -1), (-1, 1), (1, -1), (1, 1))
BACK = (1, 0, 3, 2, 7, 6, 5, 4)
GELU_A = math.sqrt(2.0 / math.pi)
GELU_B = 0.044715
NT = (((1,), (1,)), ((), ()))
TN = (((0,), (0,)), ((), ()))


def conv_rows(pad, taps, row0, flip):
    halves = []
    for h in range(2):
        acc = jnp.zeros((CONV_ROWS, W, 128), F32)
        for j in range(7):
            window = pad[h, pl.ds(row0, CONV_ROWS + 6), LEFT - 3 + j : LEFT - 3 + j + W, :]
            for i in range(7):
                ti, tj = (6 - i, 6 - j) if flip else (i, j)
                tap = taps[ti, tj : tj + 1, h * 128 : (h + 1) * 128]
                acc = acc + tap[None] * window[i : i + CONV_ROWS]
        halves.append(acc.reshape(CONV_ROWS * W, 128))
    return jnp.concatenate(halves, axis=-1)


def body(
    scale,
    saved, og, tissue, taps, cbias, gain, nbias, w_in, b_in, w_out, lscale,
    out, gi_out, go_out, taps_out,
    xpad, gpad, std, inv, nbuf, hbuf, dgelu, bgb, pgb, gin, cgt,
    col_s, row_r, col_r, cor_r,
    s0i, s0o, r0i, r0o, t1i, t1o, r1i, r1o, p2i, p2o, r2i, r2o, r3,
    tacc, ts0, tr0, try_, trz, tfin,
    halo_send, halo_recv, shift_send, shift_recv,
    sib_send, sib_recv, a_send, a_recv, b_send, b_recv,
    c_send, c_recv, d_send, d_recv, e_send, e_recv, ty_send, ty_recv, tz_send, tz_recv,
):
    seg = lax.axis_index("segment")
    r = lax.axis_index("row")
    c = lax.axis_index("col")
    core = lax.rem(c, 2)
    y = lax.div(c, 2)
    sib = (seg, r, c + 1 - 2 * core)
    off_c = c + 2 * core - 1
    off_ok = jnp.logical_and(off_c >= 0, off_c < COLS)

    def near_ok(d):
        dr, dc = DIRS[d]
        ok = None
        if dr:
            ok = (r > 0) if dr < 0 else (r < ROWS - 1)
        if dc:
            okc = (c > 0) if dc < 0 else (c < COLS - 1)
            ok = okc if ok is None else jnp.logical_and(ok, okc)
        return ok

    def near_id(d):
        dr, dc = DIRS[d]
        return (seg, r + dr, c + dc)

    def zpeer(k):
        return lax.rem(r + k, ROWS)

    def ypeer(k):
        return lax.rem(y + k, YS)

    barrier = pltpu.get_barrier_semaphore()

    def greet(device):
        pl.semaphore_signal(barrier, inc=1, device_id=device, device_id_type=MESH)

    greet(sib)
    count = 1 + 2 * 7
    for k in range(1, 8):
        greet((seg, zpeer(k), c))
        greet((seg, r, 2 * ypeer(k) + core))

    @pl.when(off_ok)
    def _():
        greet((seg, r, off_c))

    count = count + jnp.where(off_ok, 1, 0)
    for d in range(4, 8):
        ok = near_ok(d)

        @pl.when(ok)
        def _(d=d):
            greet(near_id(d))

        count = count + jnp.where(ok, 1, 0)

    @pl.when(seg > 0)
    def _():
        greet((seg - 1, r, c))

    @pl.when(seg < SEGS - 1)
    def _():
        greet((seg + 1, r, c))

    count = count + jnp.where(seg > 0, 1, 0) + jnp.where(seg < SEGS - 1, 1, 0)

    def stage_cols(pad, p):
        for h in range(2):
            lanes = slice(h * 128, (h + 1) * 128)
            col_s[p, 0, :, :, lanes] = pad[h, 3 : 3 + H, LEFT : LEFT + 3, :].astype(BF16)
            col_s[p, 1, :, :, lanes] = pad[h, 3 : 3 + H, LEFT + W - 3 : LEFT + W, :].astype(BF16)

    for h in range(2):
        xpad[h, 3 : 3 + H, LEFT : LEFT + W, :] = saved[:, :, h * 128 : (h + 1) * 128].astype(F32)
    stage_cols(xpad, 0)

    def landing(p, d):
        if d < 2:
            return row_r.at[p, d]
        if d < 4:
            return col_r.at[p, d - 2]
        return cor_r.at[p, d - 4]

    for p in range(2):
        for d in range(8):

            @pl.when(jnp.logical_not(near_ok(d)))
            def _(p=p, d=d):
                ref = landing(p, d)
                ref[...] = jnp.zeros(ref.shape, BF16)

    pl.semaphore_wait(barrier, count)

    def halo_copy(p, tile, d):
        dr, dc = DIRS[d]
        rows = slice(0, 3) if dr < 0 else slice(H - 3, H)
        if dc == 0:
            src = tile.at[rows]
        elif dr == 0:
            src = col_s.at[p, 0 if dc < 0 else 1]
        else:
            src = col_s.at[p, 0 if dc < 0 else 1, rows]
        return pltpu.make_async_remote_copy(
            src_ref=src,
            dst_ref=landing(p, BACK[d]),
            send_sem=halo_send.at[p, d],
            recv_sem=halo_recv.at[p, BACK[d]],
            device_id=near_id(d),
            device_id_type=MESH,
        )

    def halo_start(p, tile):
        for d in (4, 5, 6, 7, 0, 1, 2, 3):

            @pl.when(near_ok(d))
            def _(d=d):
                halo_copy(p, tile, d).start()

    def halo_wait(p, tile):
        for d in range(8):

            @pl.when(near_ok(d))
            def _(d=d):
                pltpu.make_async_remote_copy(
                    src_ref=landing(p, d),
                    dst_ref=landing(p, d),
                    send_sem=halo_send.at[p, d],
                    recv_sem=halo_recv.at[p, d],
                    device_id=near_id(d),
                    device_id_type=MESH,
                ).wait_recv()

    def halo_drain(p, tile):
        for d in range(8):

            @pl.when(near_ok(d))
            def _(d=d):
                halo_copy(p, tile, d).wait_send()

    def unpack(pad, p):
        for h in range(2):
            lanes = slice(h * 128, (h + 1) * 128)
            lo, hi = slice(LEFT - 3, LEFT), slice(LEFT + W, LEFT + W + 3)
            pad[h, 0:3, LEFT : LEFT + W, :] = row_r[p, 0, :, :, lanes].astype(F32)
            pad[h, 3 + H : 6 + H, LEFT : LEFT + W, :] = row_r[p, 1, :, :, lanes].astype(F32)
            pad[h, 3 : 3 + H, lo, :] = col_r[p, 0, :, :, lanes].astype(F32)
            pad[h, 3 : 3 + H, hi, :] = col_r[p, 1, :, :, lanes].astype(F32)
            pad[h, 0:3, lo, :] = cor_r[p, 0, :, :, lanes].astype(F32)
            pad[h, 0:3, hi, :] = cor_r[p, 1, :, :, lanes].astype(F32)
            pad[h, 3 + H : 6 + H, lo, :] = cor_r[p, 2, :, :, lanes].astype(F32)
            pad[h, 3 + H : 6 + H, hi, :] = cor_r[p, 3, :, :, lanes].astype(F32)

    halo_start(0, saved)
    halo_wait(0, saved)
    unpack(xpad, 0)

    @pl.loop(0, H // CONV_ROWS)
    def _(n):
        conv = conv_rows(xpad, taps, n * CONV_ROWS, False) + cbias[...]
        pix = pl.ds(pl.multiple_of(n * (CONV_ROWS * W), CONV_ROWS * W), CONV_ROWS * W)
        centred = conv - jnp.mean(conv, axis=-1, keepdims=True)
        inv_std = lax.rsqrt(jnp.mean(centred * centred, axis=-1, keepdims=True) + EPS)
        standard = centred * inv_std
        std[pix, :] = standard
        inv[pix, :] = jnp.broadcast_to(inv_std, (CONV_ROWS * W, 128))
        nbuf[pix, :] = (standard * gain[...] + nbias[...]).astype(BF16)

    @pl.loop(0, HID // 256)
    def _(n):
        units = pl.ds(pl.multiple_of(n * 256, 256), 256)
        pre = jnp.dot(nbuf[...], w_in[:, units], preferred_element_type=F32) + b_in[:, units]
        square = pre * pre
        th = jnp.tanh(GELU_A * (pre + GELU_B * (square * pre)))
        half = 0.5 * (1.0 + th)
        hbuf[:, units] = (pre * half).astype(BF16)
        slope = GELU_A * (1.0 + (3.0 * GELU_B) * square)
        dgelu[:, units] = half + 0.5 * pre * (1.0 - th * th) * slope

    def shift_copy(src, n):
        rows = pl.ds(n * CH_ROWS, CH_ROWS)
        return pltpu.make_async_remote_copy(
            src_ref=src.at[rows],
            dst_ref=gin.at[rows],
            send_sem=shift_send.at[n],
            recv_sem=shift_recv.at[n],
            device_id=(lax.rem(seg + SEGS - 1, SEGS), r, c),
            device_id_type=MESH,
        )

    mask = tissue[0, 0].astype(F32)

    @pl.when(seg == SEGS - 1)
    def _():
        gin[...] = og[...]

    for n in range(CHUNKS):

        @pl.when(seg < SEGS - 1)
        def _(n=n):
            shift_copy(out, n).wait_recv()

        rows = slice(n * CH_ROWS, (n + 1) * CH_ROWS)
        pix = slice(n * CH_PIX, (n + 1) * CH_PIX)
        upstream = gin[rows].reshape(CH_PIX, C).astype(F32)
        bg = (mask * lscale[...] * upstream).astype(BF16)
        bgb[pix, :] = bg
        hidden_grad = lax.dot_general(bg, w_out[...], NT, preferred_element_type=F32)
        pg = (hidden_grad * dgelu[pix, :]).astype(BF16)
        pgb[pix, :] = pg
        ng = lax.dot_general(pg, w_in[...], NT, preferred_element_type=F32) * gain[...]
        standard = std[pix, :]
        m1 = jnp.mean(ng, axis=-1, keepdims=True)
        m2 = jnp.mean(ng * standard, axis=-1, keepdims=True)
        cg = (inv[pix, 0:1] * (ng - m1 - standard * m2)).astype(BF16)
        cgt[rows] = cg.reshape(CH_ROWS, W, C)
        wide = cg.astype(F32).reshape(CH_ROWS, W, C)
        for h in range(2):
            gpad[h, 3 + n * CH_ROWS : 3 + (n + 1) * CH_ROWS, LEFT : LEFT + W, :] = wide[:, :, h * 128 : (h + 1) * 128]
    stage_cols(gpad, 1)
    halo_start(1, cgt)

    for n in range(HID // 256):
        units = slice(n * 256, (n + 1) * 256)
        gi = lax.dot_general(nbuf[...], pgb[:, units], TN, preferred_element_type=F32) * scale
        go = lax.dot_general(hbuf[:, units], bgb[...], TN, preferred_element_type=F32) * scale
        gi = gi.astype(BF16)
        go = go.astype(BF16)
        for k in range(COLS):
            s0i[k % 2, k // 2, :, units] = gi[16 * k : 16 * k + 16]
        for k in range(4):
            owner = n * 4 + k
            s0o[owner % 2, owner // 2] = go[64 * k : 64 * k + 64]

    def sib_copy(src, dst, k):
        return pltpu.make_async_remote_copy(
            src_ref=src, dst_ref=dst, send_sem=sib_send.at[k], recv_sem=sib_recv.at[k],
            device_id=sib, device_id_type=MESH,
        )

    other = 1 - core
    first_i = sib_copy(s0i.at[other], r0i, 0)
    first_o = sib_copy(s0o.at[other], r0o, 1)
    first_i.start()
    first_o.start()

    halo_wait(1, cgt)
    unpack(gpad, 1)
    for n in range(CHUNKS):
        for m in range(CH_ROWS // CONV_ROWS):
            row0 = n * CH_ROWS + m * CONV_ROWS
            total = conv_rows(gpad, taps, row0, True).reshape(CONV_ROWS, W, C)
            total = gin[row0 : row0 + CONV_ROWS].astype(F32) + total
            out[row0 : row0 + CONV_ROWS] = total.astype(BF16)

        @pl.when(seg > 0)
        def _(n=n):
            shift_copy(out, n).start()

    def remote(src, dst, send, recv, device):
        return pltpu.make_async_remote_copy(
            src_ref=src, dst_ref=dst, send_sem=send, recv_sem=recv,
            device_id=device, device_id_type=MESH,
        )

    first_i.wait()
    for k in range(YS):
        t1i[k] = (s0i[core, k].astype(F32) + r0i[k].astype(F32)).astype(BF16)

    def a_copy(k):
        p = ypeer(k)
        return remote(t1i.at[p], r1i.at[k - 1], a_send.at[k - 1], a_recv.at[k - 1], (seg, r, 2 * p + core))

    for k in range(1, 8):
        a_copy(k).start()
    first_o.wait()
    for k in range(YS):
        both = s0o[core, k].astype(F32) + r0o[k].astype(F32)
        both = both.astype(BF16)
        for q in range(ROWS):
            t1o[q, k] = both[16 * (q // 2) : 16 * (q // 2) + 16, 128 * (q % 2) : 128 * (q % 2) + 128]

    def b_copy(k):
        p = zpeer(k)
        return remote(t1o.at[p], r1o.at[k - 1], b_send.at[k - 1], b_recv.at[k - 1], (seg, p, c))

    for k in range(1, 8):
        b_copy(k).start()

    for h in range(2):
        for j in range(7):
            sums = [jnp.zeros((8, 128), F32) for _ in range(7)]
            for block in range(H // CONV_ROWS):
                row0 = block * CONV_ROWS
                window = xpad[h, row0 : row0 + CONV_ROWS + 6, LEFT - 3 + j : LEFT - 3 + j + W, :]
                grad = gpad[h, 3 + row0 : 3 + row0 + CONV_ROWS, LEFT : LEFT + W, :]
                for i in range(7):
                    prod = (window[i : i + CONV_ROWS] * grad).reshape(2 * CONV_ROWS, 8, 128)
                    sums[i] = sums[i] + jnp.sum(prod, axis=0)
            for i in range(7):
                tacc[h, 7 * i + j] = sums[i]
    for h in range(2):
        ts0[h] = jnp.zeros((64, 128), BF16)
        ts0[h, 0:49] = (jnp.sum(tacc[h], axis=1) * scale).astype(BF16)
    tap_a = sib_copy(ts0.at[other], tr0, 2)
    tap_a.start()

    for k in range(1, 8):
        a_copy(k).wait_recv()
    mine = t1i[y].astype(F32)
    for k in range(7):
        mine = mine + r1i[k].astype(F32)
    mine = mine.astype(BF16)
    for q in range(ROWS):
        p2i[q] = mine[:, 128 * q : 128 * q + 128]

    def c_copy(k):
        p = zpeer(k)
        return remote(p2i.at[p], r2i.at[k - 1], c_send.at[k - 1], c_recv.at[k - 1], (seg, p, c))

    for k in range(1, 8):
        c_copy(k).start()

    tap_a.wait()
    try_[y] = (ts0[core].astype(F32) + tr0[...].astype(F32)).astype(BF16)

    def ty_copy(k):
        return remote(try_.at[y], try_.at[y], ty_send.at[k - 1], ty_recv.at[y], (seg, r, 2 * ypeer(k) + core))

    def ty_landed(k):
        p = ypeer(k)
        return remote(try_.at[p], try_.at[p], ty_send.at[k - 1], ty_recv.at[p], (seg, r, 2 * p + core))

    for k in range(1, 8):
        ty_copy(k).start()

    for k in range(1, 8):
        b_copy(k).wait_recv()
    part = t1o[r].astype(F32)
    for k in range(7):
        part = part + r1o[k].astype(F32)
    p2o[...] = part.astype(BF16)

    def d_copy(k):
        p = ypeer(k)
        return remote(p2o.at[p], r2o.at[k - 1], d_send.at[k - 1], d_recv.at[k - 1], (seg, r, 2 * p + core))

    for k in range(1, 8):
        d_copy(k).start()

    for k in range(1, 8):
        ty_landed(k).wait_recv()
    tsum = try_[0].astype(F32)
    for k in range(1, 8):
        tsum = tsum + try_[k].astype(F32)
    trz[r] = tsum.astype(BF16)

    def tz_copy(k):
        return remote(trz.at[r], trz.at[r], tz_send.at[k - 1], tz_recv.at[r], (seg, zpeer(k), c))

    def tz_landed(k):
        p = zpeer(k)
        return remote(trz.at[p], trz.at[p], tz_send.at[k - 1], tz_recv.at[p], (seg, p, c))

    for k in range(1, 8):
        tz_copy(k).start()

    for k in range(1, 8):
        c_copy(k).wait_recv()
    full_i = p2i[r].astype(F32)
    for k in range(7):
        full_i = full_i + r2i[k].astype(F32)
    for k in range(1, 8):
        d_copy(k).wait_recv()
    full_o = p2o[y].astype(F32)
    for k in range(7):
        full_o = full_o + r2o[k].astype(F32)
    r3[r, 0] = full_i
    r3[r, 1] = full_o

    def e_copy(k):
        return remote(r3.at[r], r3.at[r], e_send.at[k - 1], e_recv.at[r], (seg, zpeer(k), c))

    def e_landed(k):
        p = zpeer(k)
        return remote(r3.at[p], r3.at[p], e_send.at[k - 1], e_recv.at[p], (seg, p, c))

    for k in range(1, 8):
        e_copy(k).start()

    for k in range(1, 8):
        tz_landed(k).wait_recv()
    tsum = trz[0].astype(F32)
    for k in range(1, 8):
        tsum = tsum + trz[k].astype(F32)
    tfin[core] = tsum
    tap_b = sib_copy(tfin.at[core], tfin.at[core], 3)
    tap_b.start()

    for k in range(1, 8):
        e_landed(k).wait_recv()
    for q in range(ROWS):
        gi_out[:, 128 * q : 128 * q + 128] = r3[q, 0]
        go_out[16 * (q // 2) : 16 * (q // 2) + 16, 128 * (q % 2) : 128 * (q % 2) + 128] = r3[q, 1]

    tap_b.wait_send()
    sib_copy(tfin.at[other], tfin.at[other], 3).wait_recv()
    for h in range(2):
        for i in range(7):
            taps_out[i, :, h * 128 : (h + 1) * 128] = tfin[h, 7 * i : 7 * i + 7, :]

    halo_drain(0, saved)
    halo_drain(1, cgt)
    for n in range(CHUNKS):

        @pl.when(seg > 0)
        def _(n=n):
            shift_copy(out, n).wait_send()

    for k in range(1, 8):
        for copy in (a_copy, b_copy, c_copy, d_copy, e_copy, ty_copy, tz_copy):
            copy(k).wait_send()


def per_device(
    saved_inputs, out_grad, tissue, conv_taps, conv_bias, norm_gain, norm_bias,
    w_in, b_in, w_out, layer_scale,
):
    scale = 1.0 / math.sqrt(ROWS * H * COLS * W)
    vmem = pl.BlockSpec(memory_space=pltpu.VMEM)
    smem = pl.BlockSpec(memory_space=pltpu.SMEM)
    dma = pltpu.SemaphoreType.DMA
    px = H * W
    out, gi, go, gt = pl.pallas_call(
        functools.partial(body, scale),
        out_shape=(
            jax.ShapeDtypeStruct((H, W, C), BF16),
            jax.ShapeDtypeStruct((C // COLS, HID), F32),
            jax.ShapeDtypeStruct((HID // COLS, C), F32),
            jax.ShapeDtypeStruct((7, 7, C), F32),
        ),
        in_specs=[vmem, vmem, smem] + [vmem] * 8,
        out_specs=(vmem, vmem, vmem, vmem),
        scratch_shapes=[
            pltpu.VMEM((2, H + 6, PADW, 128), F32),
            pltpu.VMEM((2, H + 6, PADW, 128), F32),
            pltpu.VMEM((px, C), F32),
            pltpu.VMEM((px, 128), F32),
            pltpu.VMEM((px, C), BF16),
            pltpu.VMEM((px, HID), BF16),
            pltpu.VMEM((px, HID), F32),
            pltpu.VMEM((px, C), BF16),
            pltpu.VMEM((px, HID), BF16),
            pltpu.VMEM((H, W, C), BF16),
            pltpu.VMEM((H, W, C), BF16),
            pltpu.VMEM((2, 2, H, 3, C), BF16),
            pltpu.VMEM((2, 2, 3, W, C), BF16),
            pltpu.VMEM((2, 2, H, 3, C), BF16),
            pltpu.VMEM((2, 4, 3, 3, C), BF16),
            pltpu.VMEM((2, YS, 16, HID), BF16),
            pltpu.VMEM((2, YS, 64, C), BF16),
            pltpu.VMEM((YS, 16, HID), BF16),
            pltpu.VMEM((YS, 64, C), BF16),
            pltpu.VMEM((YS, 16, HID), BF16),
            pltpu.VMEM((ROWS, YS, 16, 128), BF16),
            pltpu.VMEM((7, 16, HID), BF16),
            pltpu.VMEM((7, YS, 16, 128), BF16),
            pltpu.VMEM((ROWS, 16, 128), BF16),
            pltpu.VMEM((YS, 16, 128), BF16),
            pltpu.VMEM((7, 16, 128), BF16),
            pltpu.VMEM((7, 16, 128), BF16),
            pltpu.VMEM((ROWS, 2, 16, 128), F32),
            pltpu.VMEM((2, 49, 8, 128), F32),
            pltpu.VMEM((2, 64, 128), BF16),
            pltpu.VMEM((64, 128), BF16),
            pltpu.VMEM((YS, 64, 128), BF16),
            pltpu.VMEM((ROWS, 64, 128), BF16),
            pltpu.VMEM((2, 64, 128), F32),
            dma((2, 8)), dma((2, 8)), dma((CHUNKS,)), dma((CHUNKS,)),
            dma((4,)), dma((4,)),
            dma((7,)), dma((7,)), dma((7,)), dma((7,)),
            dma((7,)), dma((7,)), dma((7,)), dma((7,)),
            dma((7,)), dma((8,)), dma((7,)), dma((8,)), dma((7,)), dma((8,)),
        ],
        compiler_params=pltpu.CompilerParams(collective_id=0, has_side_effects=True),
    )(
        saved_inputs[0, 0], out_grad[0], tissue[0], conv_taps[0], conv_bias, norm_gain, norm_bias,
        w_in[0], b_in, w_out[0], layer_scale,
    )
    return (out[None, None], gi[None], go[None], gt[None])


def solution(mesh):
    return jax.shard_map(
        per_device,
        mesh=mesh,
        in_specs=(
            P("segment", None, "row", "col", None),
            P(None, "row", "col", None),
            P(None, "row", "col"),
            P("segment", None, None, None),
            P("segment", None),
            P("segment", None),
            P("segment", None),
            P("segment", None, None),
            P("segment", None),
            P("segment", None, None),
            P("segment", None),
        ),
        out_specs=(
            P("segment", None, "row", "col", None),
            P("segment", "col", None),
            P("segment", "col", None),
            P("segment", None, None, None),
        ),
        check_vma=False,
    )
```

```python
import functools
import math

import jax
import jax.numpy as jnp
from jax import lax
from jax.experimental import pallas as pl
from jax.experimental.pallas import tpu as pltpu
from jax.sharding import PartitionSpec as P

F32 = jnp.float32
BF16 = jnp.bfloat16
MESH = pl.DeviceIdType.MESH
EPS = 1e-06
VMEM_MAIN = 28 * 1024 * 1024
H = 16
W = 16
C = 256
HID = 1024
ROWS = 8
COLS = 16
YS = 8
SEGS = 4
LEFT = 8
PADW = 32
CONV_ROWS = 4
ORDER = (0, 12, 4, 8)
CHUNKS = len(ORDER)
CH_PIX = CONV_ROWS * W
DIRS = ((-1, 0), (1, 0), (0, -1), (0, 1), (-1, -1), (-1, 1), (1, -1), (1, 1))
BACK = (1, 0, 3, 2, 7, 6, 5, 4)
FAR = (4, 3, 5, 2, 6, 1, 7)
GELU_A = math.sqrt(2.0 / math.pi)
GELU_B = 0.044715
NT = (((1,), (1,)), ((), ()))
TN = (((0,), (0,)), ((), ()))


def conv_rows(pad, taps, row0, flip):
    halves = []
    for h in range(2):
        acc = jnp.zeros((CONV_ROWS, W, 128), F32)
        for j in range(7):
            window = pad[h, pl.ds(row0, CONV_ROWS + 6), LEFT - 3 + j : LEFT - 3 + j + W, :]
            for i in range(7):
                ti, tj = (6 - i, 6 - j) if flip else (i, j)
                tap = taps[ti, tj, :, h * 128 : (h + 1) * 128]
                acc = acc + tap[None] * window[i : i + CONV_ROWS]
        halves.append(acc.reshape(CONV_ROWS * W, 128))
    return jnp.concatenate(halves, axis=-1)


def body(
    scale,
    saved_h, og_h, tissue_h, taps_h, cbias_h, gain_h, nbias_h, w_in_h, b_in_h, w_out_h, lscale_h,
    out, gi_out, go_out, taps_out,
    saved, og, tissue, taps, cbias, gain, nbias, w_in, b_in, w_out, lscale, load_sem, tbuf, htbuf,
    xpad, gpad, std, inv, nbuf, hbuf, dgelu, bgb, pgb, gin, cgt,
    col_s, row_r, col_r, cor_r, strip, corner,
    s0i, s0o, r0i, r0o, t1i, t1o, r1i, r1o, p2i, p2o, r2i, r2o, r3,
    tacc, ts0, tr0, try_, trz, tfin,
    halo_send, halo_recv, shift_send, shift_recv,
    sib_send, sib_recv, a_send, a_recv, b_send, b_recv,
    c_send, c_recv, d_send, d_recv, e_send, e_recv, ty_send, ty_recv, tz_send, tz_recv,
):
    seg = lax.axis_index("segment")
    r = lax.axis_index("row")
    c = lax.axis_index("col")
    core = lax.rem(c, 2)
    y = lax.div(c, 2)
    sib = (seg, r, c + 1 - 2 * core)
    off_c = c + 2 * core - 1
    off_ok = jnp.logical_and(off_c >= 0, off_c < COLS)

    def near_ok(d):
        dr, dc = DIRS[d]
        ok = None
        if dr:
            ok = (r > 0) if dr < 0 else (r < ROWS - 1)
        if dc:
            okc = (c > 0) if dc < 0 else (c < COLS - 1)
            ok = okc if ok is None else jnp.logical_and(ok, okc)
        return ok

    def near_id(d):
        dr, dc = DIRS[d]
        return (seg, r + dr, c + dc)

    def zpeer(k):
        return lax.rem(r + k, ROWS)

    def ypeer(k):
        return lax.rem(y + k, YS)

    barrier = pltpu.get_barrier_semaphore()

    def greet(device):
        pl.semaphore_signal(barrier, inc=1, device_id=device, device_id_type=MESH)

    greet(sib)
    count = 1 + 2 * 7
    for k in range(1, 8):
        greet((seg, zpeer(k), c))
        greet((seg, r, 2 * ypeer(k) + core))

    @pl.when(off_ok)
    def _():
        greet((seg, r, off_c))

    count = count + jnp.where(off_ok, 1, 0)
    for d in range(4, 8):
        ok = near_ok(d)

        @pl.when(ok)
        def _(d=d):
            greet(near_id(d))

        count = count + jnp.where(ok, 1, 0)

    @pl.when(seg > 0)
    def _():
        greet((seg - 1, r, c))

    @pl.when(seg < SEGS - 1)
    def _():
        greet((seg + 1, r, c))

    count = count + jnp.where(seg > 0, 1, 0) + jnp.where(seg < SEGS - 1, 1, 0)

    sources = (saved_h, taps_h, cbias_h, gain_h, nbias_h, w_in_h, b_in_h, w_out_h, lscale_h, tissue_h, og_h)
    places = (saved, taps, cbias, gain, nbias, w_in, b_in, w_out, lscale, tissue, og)
    loads = [pltpu.make_async_copy(a, b, load_sem.at[n]) for n, (a, b) in enumerate(zip(sources, places))]
    for load in loads:
        load.start()

    def stage_cols(pad, p, row0):
        piece = slice(4 * row0, 4 * row0 + 16)
        for side, first in ((0, LEFT), (1, LEFT + W - 4)):
            for h in range(2):
                for q in range(row0, row0 + CONV_ROWS):
                    strip[side, 4 * q : 4 * q + 4, h * 128 : (h + 1) * 128] = pad[h, 3 + q, first : first + 4, :]
            col_s[p, side, piece] = strip[side, piece].astype(BF16)

    loads[0].wait()
    for h in range(2):
        xpad[h, 3 : 3 + H, LEFT : LEFT + W, :] = saved[:, :, h * 128 : (h + 1) * 128].astype(F32)
    for row0 in ORDER:
        stage_cols(xpad, 0, row0)

    def landing(p, d, m=0):
        if d < 2:
            return row_r.at[p, d]
        if d < 4:
            return col_r.at[p, d - 2, pl.ds(16 * m, 16)]
        return cor_r.at[p, d - 4]

    def slot(d, m=0):
        return d if d not in (2, 3) else 8 + 4 * (d - 2) + m

    for p in range(2):
        for d in range(8):

            @pl.when(jnp.logical_not(near_ok(d)))
            def _(p=p, d=d):
                for m in range(4 if d in (2, 3) else 1):
                    ref = landing(p, d, m)
                    ref[...] = jnp.zeros(ref.shape, BF16)

    pl.semaphore_wait(barrier, count)

    def halo_copy(p, tile, d, m=0):
        dr, dc = DIRS[d]
        side = 0 if dc < 0 else 1
        if dc == 0:
            src = tile.at[0:3] if dr < 0 else tile.at[H - 3 : H]
        elif dr == 0:
            src = col_s.at[p, side, pl.ds(16 * m, 16)]
        else:
            src = col_s.at[p, side, pl.ds(0 if dr < 0 else 4 * H - 16, 16)]
        return pltpu.make_async_remote_copy(
            src_ref=src,
            dst_ref=landing(p, BACK[d], m),
            send_sem=halo_send.at[p, slot(d, m)],
            recv_sem=halo_recv.at[p, slot(BACK[d], m)],
            device_id=near_id(d),
            device_id_type=MESH,
        )

    def messages(row0):
        m = row0 // CONV_ROWS
        edge = ((4, 0), (5, 0), (0, 0)) if row0 == 0 else ((6, 0), (7, 0), (1, 0)) if row0 == H - CONV_ROWS else ()
        return edge + ((2, m), (3, m))

    def halo_start(p, tile, row0):
        for d, m in messages(row0):

            @pl.when(near_ok(d))
            def _(d=d, m=m):
                halo_copy(p, tile, d, m).start()

    def halo_wait(p, row0):
        for d, m in messages(row0):

            @pl.when(near_ok(d))
            def _(d=d, m=m):
                pltpu.make_async_remote_copy(
                    src_ref=landing(p, d, m),
                    dst_ref=landing(p, d, m),
                    send_sem=halo_send.at[p, slot(d, m)],
                    recv_sem=halo_recv.at[p, slot(d, m)],
                    device_id=near_id(d),
                    device_id_type=MESH,
                ).wait_recv()

    def halo_drain(p, tile):
        for row0 in ORDER:
            for d, m in messages(row0):

                @pl.when(near_ok(d))
                def _(d=d, m=m):
                    halo_copy(p, tile, d, m).wait_send()

    def unpack(pad, p, row0):
        piece = slice(4 * row0, 4 * row0 + 16)
        for side, first in ((0, LEFT - 4), (1, LEFT + W)):
            strip[side, piece] = col_r[p, side, piece].astype(F32)
            for h in range(2):
                for q in range(row0, row0 + CONV_ROWS):
                    pad[h, 3 + q, first : first + 4, :] = strip[side, 4 * q : 4 * q + 4, h * 128 : (h + 1) * 128]
        if row0 not in (0, H - CONV_ROWS):
            return
        top = row0 == 0
        base, src0 = (0, 1) if top else (3 + H, 0)
        for side, first in ((0, LEFT - 4), (1, LEFT + W)):
            k = side + (0 if top else 2)
            corner[k] = cor_r[p, k].astype(F32)
            for h in range(2):
                for q in range(3):
                    m = 4 * (src0 + q)
                    pad[h, base + q, first : first + 4, :] = corner[k, m : m + 4, h * 128 : (h + 1) * 128]
        for h in range(2):
            lanes = slice(h * 128, (h + 1) * 128)
            pad[h, base : base + 3, LEFT : LEFT + W, :] = row_r[p, 0 if top else 1, :, :, lanes].astype(F32)

    for row0 in ORDER:
        halo_start(0, saved, row0)
    for load in loads[1:]:
        load.wait()
    for row0 in ORDER:
        halo_wait(0, row0)
        unpack(xpad, 0, row0)

    @pl.loop(0, H // CONV_ROWS)
    def _(n):
        conv = conv_rows(xpad, taps, n * CONV_ROWS, False) + cbias[...]
        pix = pl.ds(pl.multiple_of(n * (CONV_ROWS * W), CONV_ROWS * W), CONV_ROWS * W)
        centred = conv - jnp.mean(conv, axis=-1, keepdims=True)
        inv_std = lax.rsqrt(jnp.mean(centred * centred, axis=-1, keepdims=True) + EPS)
        standard = centred * inv_std
        std[pix, :] = standard
        inv[pix, :] = jnp.broadcast_to(inv_std, (CONV_ROWS * W, 128))
        nbuf[pix, :] = (standard * gain[...] + nbias[...]).astype(BF16)

    @pl.loop(0, HID // 256)
    def _(n):
        units = pl.ds(pl.multiple_of(n * 256, 256), 256)
        pre = jnp.dot(nbuf[...], w_in[:, units], preferred_element_type=F32) + b_in[:, units]
        square = pre * pre
        th = jnp.tanh(GELU_A * (pre + GELU_B * (square * pre)))
        half = 0.5 * (1.0 + th)
        hbuf[:, units] = (pre * half).astype(BF16)
        slope = GELU_A * (1.0 + (3.0 * GELU_B) * square)
        dgelu[:, units] = half + 0.5 * pre * (1.0 - th * th) * slope

    def shift_copy(src, n):
        rows = pl.ds(ORDER[n], CONV_ROWS)
        return pltpu.make_async_remote_copy(
            src_ref=src.at[rows],
            dst_ref=gin.at[rows],
            send_sem=shift_send.at[n],
            recv_sem=shift_recv.at[n],
            device_id=(lax.rem(seg + SEGS - 1, SEGS), r, c),
            device_id_type=MESH,
        )

    mask = tissue[...].astype(F32)

    def turn():
        tbuf[...] = nbuf[...].T
        for n in range(HID // 256):
            htbuf[n * 256 : (n + 1) * 256, :] = hbuf[:, n * 256 : (n + 1) * 256].T

    @pl.when(seg == SEGS - 1)
    def _():
        gin[...] = og[...]

    @pl.when(seg < SEGS - 1)
    def _():
        turn()

    for n, row0 in enumerate(ORDER):

        @pl.when(seg < SEGS - 1)
        def _(n=n):
            shift_copy(out, n).wait_recv()

        rows = slice(row0, row0 + CONV_ROWS)
        pix = slice(row0 * W, row0 * W + CH_PIX)
        upstream = gin[rows].reshape(CH_PIX, C).astype(F32)
        bg = (mask * lscale[...] * upstream).astype(BF16)
        bgb[pix, :] = bg
        hidden_grad = lax.dot_general(bg, w_out[...], NT, preferred_element_type=F32)
        pg = (hidden_grad * dgelu[pix, :]).astype(BF16)
        pgb[pix, :] = pg
        ng = lax.dot_general(pg, w_in[...], NT, preferred_element_type=F32) * gain[...]
        standard = std[pix, :]
        m1 = jnp.mean(ng, axis=-1, keepdims=True)
        m2 = jnp.mean(ng * standard, axis=-1, keepdims=True)
        cg = (inv[pix, 0:1] * (ng - m1 - standard * m2)).astype(BF16)
        cgt[rows] = cg.reshape(CONV_ROWS, W, C)
        wide = cg.astype(F32).reshape(CONV_ROWS, W, C)
        for h in range(2):
            gpad[h, 3 + row0 : 3 + row0 + CONV_ROWS, LEFT : LEFT + W, :] = wide[:, :, h * 128 : (h + 1) * 128]
        stage_cols(gpad, 1, row0)
        halo_start(1, cgt, row0)

    def remote(src, dst, send, recv, device):
        return pltpu.make_async_remote_copy(
            src_ref=src, dst_ref=dst, send_sem=send, recv_sem=recv,
            device_id=device, device_id_type=MESH,
        )

    def all_of(ref, send, recv):
        return remote(ref, ref, send, recv, sib)

    def sib_copy(src, dst, k):
        return remote(src, dst, sib_send.at[k], sib_recv.at[k], sib)

    other = 1 - core
    first_i = sib_copy(s0i.at[other], r0i, 0)
    first_o = sib_copy(s0o.at[other], r0o, 1)
    tap_a = sib_copy(ts0.at[other], tr0, 2)

    def gradients():
        for n in range(HID // 256):
            units = slice(n * 256, (n + 1) * 256)
            gi = jnp.dot(tbuf[...], pgb[:, units], preferred_element_type=F32) * scale
            gi = gi.astype(BF16)
            for k in range(COLS):
                s0i[k % 2, k // 2, :, units] = gi[16 * k : 16 * k + 16]
        first_i.start()
        for n in range(HID // 256):
            go = jnp.dot(htbuf[n * 256 : (n + 1) * 256, :], bgb[...], preferred_element_type=F32) * scale
            go = go.astype(BF16)
            for k in range(4):
                owner = n * 4 + k
                s0o[owner % 2, owner // 2] = go[64 * k : 64 * k + 64]
        first_o.start()
        for h in range(2):
            for j in range(7):
                sums = [jnp.zeros((8, 128), F32) for _ in range(7)]
                for block in range(H // CONV_ROWS):
                    row0 = block * CONV_ROWS
                    window = xpad[h, row0 : row0 + CONV_ROWS + 6, LEFT - 3 + j : LEFT - 3 + j + W, :]
                    grad = gpad[h, 3 + row0 : 3 + row0 + CONV_ROWS, LEFT : LEFT + W, :]
                    for i in range(7):
                        prod = (window[i : i + CONV_ROWS] * grad).reshape(2 * CONV_ROWS, 8, 128)
                        sums[i] = sums[i] + jnp.sum(prod, axis=0)
                for i in range(7):
                    tacc[h, 7 * i + j] = sums[i]
        for h in range(2):
            ts0[h] = jnp.zeros((64, 128), BF16)
            ts0[h, 0:49] = (jnp.sum(tacc[h], axis=1) * scale).astype(BF16)
        tap_a.start()

    @pl.when(seg == 0)
    def _():
        gradients()

    for n, row0 in enumerate(ORDER):
        for needed in ((0, 4), (12, 8))[n] if n < 2 else ():
            halo_wait(1, needed)
            unpack(gpad, 1, needed)
        total = conv_rows(gpad, taps, row0, True).reshape(CONV_ROWS, W, C)
        total = gin[row0 : row0 + CONV_ROWS].astype(F32) + total
        out[row0 : row0 + CONV_ROWS] = total.astype(BF16)

        @pl.when(seg > 0)
        def _(n=n):
            shift_copy(out, n).start()

    @pl.when(seg == SEGS - 1)
    def _():
        turn()

    @pl.when(seg > 0)
    def _():
        gradients()

    first_i.wait()
    for k in range(YS):
        t1i[k] = (s0i[core, k].astype(F32) + r0i[k].astype(F32)).astype(BF16)

    def a_copy(k):
        p = ypeer(k)
        return remote(t1i.at[p], r1i.at[k - 1], a_send, a_recv, (seg, r, 2 * p + core))

    for k in FAR:
        a_copy(k).start()
    first_o.wait()
    for k in range(YS):
        both = s0o[core, k].astype(F32) + r0o[k].astype(F32)
        both = both.astype(BF16)
        for q in range(ROWS):
            t1o[q, k] = both[16 * (q // 2) : 16 * (q // 2) + 16, 128 * (q % 2) : 128 * (q % 2) + 128]

    def b_copy(k):
        p = zpeer(k)
        return remote(t1o.at[p], r1o.at[k - 1], b_send, b_recv, (seg, p, c))

    for k in FAR:
        b_copy(k).start()

    tap_a.wait()
    try_[y] = (ts0[core].astype(F32) + tr0[...].astype(F32)).astype(BF16)

    def ty_copy(k):
        return remote(try_.at[y], try_.at[y], ty_send, ty_recv, (seg, r, 2 * ypeer(k) + core))

    for k in FAR:
        ty_copy(k).start()

    all_of(r1i, a_send, a_recv).wait_recv()
    mine = t1i[y].astype(F32)
    for k in range(7):
        mine = mine + r1i[k].astype(F32)
    mine = mine.astype(BF16)
    for q in range(ROWS):
        p2i[q] = mine[:, 128 * q : 128 * q + 128]

    def c_copy(k):
        p = zpeer(k)
        return remote(p2i.at[p], r2i.at[k - 1], c_send, c_recv, (seg, p, c))

    for k in FAR:
        c_copy(k).start()

    all_of(r1o, b_send, b_recv).wait_recv()
    part = t1o[r].astype(F32)
    for k in range(7):
        part = part + r1o[k].astype(F32)
    p2o[...] = part.astype(BF16)

    def d_copy(k):
        p = ypeer(k)
        return remote(p2o.at[p], r2o.at[k - 1], d_send, d_recv, (seg, r, 2 * p + core))

    for k in FAR:
        d_copy(k).start()

    all_of(try_.at[pl.ds(0, 7)], ty_send, ty_recv).wait_recv()
    tsum = try_[0].astype(F32)
    for k in range(1, 8):
        tsum = tsum + try_[k].astype(F32)
    trz[r] = tsum.astype(BF16)

    def tz_copy(k):
        return remote(trz.at[r], trz.at[r], tz_send, tz_recv, (seg, zpeer(k), c))

    for k in FAR:
        tz_copy(k).start()

    all_of(r2i, c_send, c_recv).wait_recv()
    full_i = p2i[r].astype(F32)
    for k in range(7):
        full_i = full_i + r2i[k].astype(F32)
    all_of(r2o, d_send, d_recv).wait_recv()
    full_o = p2o[y].astype(F32)
    for k in range(7):
        full_o = full_o + r2o[k].astype(F32)
    r3[r, 0] = full_i
    r3[r, 1] = full_o

    def e_copy(k):
        return remote(r3.at[r], r3.at[r], e_send, e_recv, (seg, zpeer(k), c))

    for k in FAR:
        e_copy(k).start()

    all_of(trz.at[pl.ds(0, 7)], tz_send, tz_recv).wait_recv()
    tsum = trz[0].astype(F32)
    for k in range(1, 8):
        tsum = tsum + trz[k].astype(F32)
    tfin[core] = tsum
    tap_b = sib_copy(tfin.at[core], tfin.at[core], 3)
    tap_b.start()

    all_of(r3.at[pl.ds(0, 7)], e_send, e_recv).wait_recv()
    for q in range(ROWS):
        gi_out[:, 128 * q : 128 * q + 128] = r3[q, 0]
        go_out[16 * (q // 2) : 16 * (q // 2) + 16, 128 * (q % 2) : 128 * (q % 2) + 128] = r3[q, 1]

    tap_b.wait_send()
    sib_copy(tfin.at[other], tfin.at[other], 3).wait_recv()
    for h in range(2):
        for i in range(7):
            taps_out[i, :, 0, h * 128 : (h + 1) * 128] = tfin[h, 7 * i : 7 * i + 7, :]

    halo_drain(0, saved)
    halo_drain(1, cgt)
    for n in range(CHUNKS):

        @pl.when(seg > 0)
        def _(n=n):
            shift_copy(out, n).wait_send()

    for ref, send, recv in (
        (r1i, a_send, a_recv),
        (r1o, b_send, b_recv),
        (r2i, c_send, c_recv),
        (r2o, d_send, d_recv),
        (r3.at[pl.ds(0, 7)], e_send, e_recv),
        (try_.at[pl.ds(0, 7)], ty_send, ty_recv),
        (trz.at[pl.ds(0, 7)], tz_send, tz_recv),
    ):
        all_of(ref, send, recv).wait_send()


def place(a, b, c, d, a_out, b_out, c_out, d_out, sem):
    pairs = zip((a, b, c, d), (a_out, b_out, c_out, d_out))
    copies = [pltpu.make_async_copy(x, z, sem.at[n]) for n, (x, z) in enumerate(pairs)]
    for copy in copies:
        copy.start()
    for copy in copies:
        copy.wait()


def per_device(
    saved_inputs, out_grad, tissue, conv_taps, conv_bias, norm_gain, norm_bias,
    w_in, b_in, w_out, layer_scale,
):
    scale = 1.0 / math.sqrt(ROWS * H * COLS * W)
    vmem = pl.BlockSpec(memory_space=pltpu.VMEM)
    dma = pltpu.SemaphoreType.DMA
    px = H * W
    out, gi, go, gt = pl.pallas_call(
        functools.partial(body, scale),
        out_shape=(
            pltpu.VMEM((H, W, C), BF16),
            pltpu.VMEM((C // COLS, HID), F32),
            pltpu.VMEM((HID // COLS, C), F32),
            pltpu.VMEM((7, 7, 1, C), F32),
        ),
        in_specs=[pl.BlockSpec(memory_space=pl.ANY)] * 11,
        out_specs=(vmem, vmem, vmem, vmem),
        scratch_shapes=[
            pltpu.VMEM((H, W, C), BF16),
            pltpu.VMEM((H, W, C), BF16),
            pltpu.VMEM((1, 1), jnp.int32),
            pltpu.VMEM((7, 7, 1, C), F32),
            pltpu.VMEM((1, C), F32),
            pltpu.VMEM((1, C), F32),
            pltpu.VMEM((1, C), F32),
            pltpu.VMEM((C, HID), BF16),
            pltpu.VMEM((1, HID), F32),
            pltpu.VMEM((HID, C), BF16),
            pltpu.VMEM((1, C), F32),
            dma((11,)),
            pltpu.VMEM((C, px), BF16),
            pltpu.VMEM((HID, px), BF16),
            pltpu.VMEM((2, H + 6, PADW, 128), F32),
            pltpu.VMEM((2, H + 6, PADW, 128), F32),
            pltpu.VMEM((px, C), F32),
            pltpu.VMEM((px, 128), F32),
            pltpu.VMEM((px, C), BF16),
            pltpu.VMEM((px, HID), BF16),
            pltpu.VMEM((px, HID), F32),
            pltpu.VMEM((px, C), BF16),
            pltpu.VMEM((px, HID), BF16),
            pltpu.VMEM((H, W, C), BF16),
            pltpu.VMEM((H, W, C), BF16),
            pltpu.VMEM((2, 2, 4 * H, C), BF16),
            pltpu.VMEM((2, 2, 3, W, C), BF16),
            pltpu.VMEM((2, 2, 4 * H, C), BF16),
            pltpu.VMEM((2, 4, 16, C), BF16),
            pltpu.VMEM((2, 4 * H, C), F32),
            pltpu.VMEM((4, 16, C), F32),
            pltpu.VMEM((2, YS, 16, HID), BF16),
            pltpu.VMEM((2, YS, 64, C), BF16),
            pltpu.VMEM((YS, 16, HID), BF16),
            pltpu.VMEM((YS, 64, C), BF16),
            pltpu.VMEM((YS, 16, HID), BF16),
            pltpu.VMEM((ROWS, YS, 16, 128), BF16),
            pltpu.VMEM((7, 16, HID), BF16),
            pltpu.VMEM((7, YS, 16, 128), BF16),
            pltpu.VMEM((ROWS, 16, 128), BF16),
            pltpu.VMEM((YS, 16, 128), BF16),
            pltpu.VMEM((7, 16, 128), BF16),
            pltpu.VMEM((7, 16, 128), BF16),
            pltpu.VMEM((ROWS, 2, 16, 128), F32),
            pltpu.VMEM((2, 49, 8, 128), F32),
            pltpu.VMEM((2, 64, 128), BF16),
            pltpu.VMEM((64, 128), BF16),
            pltpu.VMEM((YS, 64, 128), BF16),
            pltpu.VMEM((ROWS, 64, 128), BF16),
            pltpu.VMEM((2, 64, 128), F32),
            dma((2, 16)), dma((2, 16)), dma((CHUNKS,)), dma((CHUNKS,)),
            dma((4,)), dma((4,)),
            dma, dma, dma, dma, dma, dma, dma, dma,
            dma, dma, dma, dma, dma, dma,
        ],
        compiler_params=pltpu.CompilerParams(collective_id=0, has_side_effects=True),
    )(*(operand for operand in (
        saved_inputs[0, 0], out_grad[0], tissue[0], conv_taps.reshape(7, 7, 1, C), conv_bias, norm_gain, norm_bias,
        w_in[0], b_in, w_out[0], layer_scale,
    )))
    results = (out, gi, go, gt)
    hbm = pl.BlockSpec(memory_space=pl.ANY)
    out, gi, go, gt = pl.pallas_call(
        place,
        out_shape=tuple(jax.ShapeDtypeStruct(a.shape, a.dtype) for a in results),
        in_specs=[vmem] * 4,
        out_specs=(hbm, hbm, hbm, hbm),
        scratch_shapes=[dma((4,))],
        compiler_params=pltpu.CompilerParams(vmem_limit_bytes=4 * 1024 * 1024),
    )(*results)
    return (out[None, None], gi[None], go[None], gt.reshape(1, 7, 7, C))


def solution(mesh):
    return jax.shard_map(
        per_device,
        mesh=mesh,
        in_specs=(
            P("segment", None, "row", "col", None),
            P(None, "row", "col", None),
            P(None, "row", "col"),
            P("segment", None, None, None),
            P("segment", None),
            P("segment", None),
            P("segment", None),
            P("segment", None, None),
            P("segment", None),
            P("segment", None, None),
            P("segment", None),
        ),
        out_specs=(
            P("segment", None, "row", "col", None),
            P("segment", "col", None),
            P("segment", "col", None),
            P("segment", None, None, None),
        ),
        check_vma=False,
    )
```

```python
import functools
import math

import jax
import jax.numpy as jnp
from jax import lax
from jax.experimental import pallas as pl
from jax.experimental.pallas import tpu as pltpu
from jax.sharding import PartitionSpec as P

F32 = jnp.float32
BF16 = jnp.bfloat16
MESH = pl.DeviceIdType.MESH
EPS = 1e-06
VMEM_MAIN = 28 * 1024 * 1024
H = 16
W = 16
C = 256
HID = 1024
ROWS = 8
COLS = 16
YS = 8
SEGS = 4
LEFT = 8
PADW = 32
CONV_ROWS = 4
ORDER = (0, 12, 4, 8)
CHUNKS = len(ORDER)
CH_PIX = CONV_ROWS * W
DIRS = ((-1, 0), (1, 0), (0, -1), (0, 1), (-1, -1), (-1, 1), (1, -1), (1, 1))
BACK = (1, 0, 3, 2, 7, 6, 5, 4)
FAR = (4, 3, 5, 2, 6, 1, 7)
GELU_A = math.sqrt(2.0 / math.pi)
GELU_B = 0.044715


def conv_rows(pad, taps, row0, flip):
    halves = []
    for h in range(2):
        acc = jnp.zeros((CONV_ROWS, W, 128), F32)
        for j in range(7):
            window = pad[h, pl.ds(row0, CONV_ROWS + 6), LEFT - 3 + j : LEFT - 3 + j + W, :]
            for i in range(7):
                ti, tj = (6 - i, 6 - j) if flip else (i, j)
                tap = taps[ti, tj, :, h * 128 : (h + 1) * 128]
                acc = acc + tap[None] * window[i : i + CONV_ROWS]
        halves.append(acc.reshape(CONV_ROWS * W, 128))
    return jnp.concatenate(halves, axis=-1)


def body(
    scale,
    saved_h, og_h, tissue_h, taps_h, cbias_h, gain_h, nbias_h, w_in_h, b_in_h, w_out_h, lscale_h,
    out, gi_out, go_out, taps_out,
    saved, og, tissue, taps, cbias, gain, nbias, w_in, b_in, w_out, lscale, load_sem, tbuf, htbuf, wo_t, wi_t,
    xpad, gpad, std, inv, nbuf, hbuf, dgelu, bgb, pgb, gin, cgt,
    col_s, row_r, col_r, cor_r, strip, corner,
    s0i, s0o, r0i, r0o, t1i, t1o, r1i, r1o, p2i, p2o, r2i, r2o, r3,
    tacc, ts0, tr0, try_, trz, tfin,
    halo_send, halo_recv, shift_send, shift_recv,
    sib_send, sib_recv, a_send, a_recv, b_send, b_recv,
    c_send, c_recv, d_send, d_recv, e_send, e_recv, ty_send, ty_recv, tz_send, tz_recv,
):
    seg = lax.axis_index("segment")
    r = lax.axis_index("row")
    c = lax.axis_index("col")
    core = lax.rem(c, 2)
    y = lax.div(c, 2)
    sib = (seg, r, c + 1 - 2 * core)
    off_c = c + 2 * core - 1
    off_ok = jnp.logical_and(off_c >= 0, off_c < COLS)

    def near_ok(d):
        dr, dc = DIRS[d]
        ok = None
        if dr:
            ok = (r > 0) if dr < 0 else (r < ROWS - 1)
        if dc:
            okc = (c > 0) if dc < 0 else (c < COLS - 1)
            ok = okc if ok is None else jnp.logical_and(ok, okc)
        return ok

    def near_id(d):
        dr, dc = DIRS[d]
        return (seg, r + dr, c + dc)

    def zpeer(k):
        return lax.rem(r + k, ROWS)

    def ypeer(k):
        return lax.rem(y + k, YS)

    sources = (saved_h, taps_h, cbias_h, gain_h, nbias_h, w_in_h, b_in_h, w_out_h, lscale_h, tissue_h, og_h)
    places = (saved, taps, cbias, gain, nbias, w_in, b_in, w_out, lscale, tissue, og)
    loads = [pltpu.make_async_copy(a, b, load_sem.at[n]) for n, (a, b) in enumerate(zip(sources, places))]
    for load in loads:
        load.start()

    barrier = pltpu.get_barrier_semaphore()

    def greet(device):
        pl.semaphore_signal(barrier, inc=1, device_id=device, device_id_type=MESH)

    greet(sib)
    count = 1 + 2 * 7
    for k in range(1, 8):
        greet((seg, zpeer(k), c))
        greet((seg, r, 2 * ypeer(k) + core))

    @pl.when(off_ok)
    def _():
        greet((seg, r, off_c))

    count = count + jnp.where(off_ok, 1, 0)
    for d in range(4, 8):
        ok = near_ok(d)

        @pl.when(ok)
        def _(d=d):
            greet(near_id(d))

        count = count + jnp.where(ok, 1, 0)

    @pl.when(seg > 0)
    def _():
        greet((seg - 1, r, c))

    @pl.when(seg < SEGS - 1)
    def _():
        greet((seg + 1, r, c))

    count = count + jnp.where(seg > 0, 1, 0) + jnp.where(seg < SEGS - 1, 1, 0)

    def stage_cols(pad, p, row0):
        piece = slice(4 * row0, 4 * row0 + 16)
        for side, first in ((0, LEFT), (1, LEFT + W - 4)):
            for h in range(2):
                for q in range(row0, row0 + CONV_ROWS):
                    strip[side, 4 * q : 4 * q + 4, h * 128 : (h + 1) * 128] = pad[h, 3 + q, first : first + 4, :]
            col_s[p, side, piece] = strip[side, piece].astype(BF16)

    loads[0].wait()
    for h in range(2):
        xpad[h, 3 : 3 + H, LEFT : LEFT + W, :] = saved[:, :, h * 128 : (h + 1) * 128].astype(F32)
    for row0 in ORDER:
        stage_cols(xpad, 0, row0)

    def landing(p, d, m=0):
        if d < 2:
            return row_r.at[p, d]
        if d < 4:
            return col_r.at[p, d - 2, pl.ds(16 * m, 16)]
        return cor_r.at[p, d - 4]

    def slot(d, m=0):
        return d if d not in (2, 3) else 8 + 4 * (d - 2) + m

    for p in range(2):
        for d in range(8):

            @pl.when(jnp.logical_not(near_ok(d)))
            def _(p=p, d=d):
                for m in range(4 if d in (2, 3) else 1):
                    ref = landing(p, d, m)
                    ref[...] = jnp.zeros(ref.shape, BF16)

    pl.semaphore_wait(barrier, count)

    def halo_copy(p, tile, d, m=0):
        dr, dc = DIRS[d]
        side = 0 if dc < 0 else 1
        if dc == 0:
            src = tile.at[0:3] if dr < 0 else tile.at[H - 3 : H]
        elif dr == 0:
            src = col_s.at[p, side, pl.ds(16 * m, 16)]
        else:
            src = col_s.at[p, side, pl.ds(0 if dr < 0 else 4 * H - 16, 16)]
        return pltpu.make_async_remote_copy(
            src_ref=src,
            dst_ref=landing(p, BACK[d], m),
            send_sem=halo_send.at[p, slot(d, m)],
            recv_sem=halo_recv.at[p, slot(BACK[d], m)],
            device_id=near_id(d),
            device_id_type=MESH,
        )

    def messages(row0):
        m = row0 // CONV_ROWS
        edge = ((4, 0), (5, 0), (0, 0)) if row0 == 0 else ((6, 0), (7, 0), (1, 0)) if row0 == H - CONV_ROWS else ()
        return edge + ((2, m), (3, m))

    def halo_start(p, tile, row0):
        for d, m in messages(row0):

            @pl.when(near_ok(d))
            def _(d=d, m=m):
                halo_copy(p, tile, d, m).start()

    def halo_wait(p, row0):
        for d, m in messages(row0):

            @pl.when(near_ok(d))
            def _(d=d, m=m):
                pltpu.make_async_remote_copy(
                    src_ref=landing(p, d, m),
                    dst_ref=landing(p, d, m),
                    send_sem=halo_send.at[p, slot(d, m)],
                    recv_sem=halo_recv.at[p, slot(d, m)],
                    device_id=near_id(d),
                    device_id_type=MESH,
                ).wait_recv()

    def halo_drain(p, tile):
        for row0 in ORDER:
            for d, m in messages(row0):

                @pl.when(near_ok(d))
                def _(d=d, m=m):
                    halo_copy(p, tile, d, m).wait_send()

    def unpack(pad, p, row0):
        piece = slice(4 * row0, 4 * row0 + 16)
        for side, first in ((0, LEFT - 4), (1, LEFT + W)):
            strip[side, piece] = col_r[p, side, piece].astype(F32)
            for h in range(2):
                for q in range(row0, row0 + CONV_ROWS):
                    pad[h, 3 + q, first : first + 4, :] = strip[side, 4 * q : 4 * q + 4, h * 128 : (h + 1) * 128]
        if row0 not in (0, H - CONV_ROWS):
            return
        top = row0 == 0
        base, src0 = (0, 1) if top else (3 + H, 0)
        for side, first in ((0, LEFT - 4), (1, LEFT + W)):
            k = side + (0 if top else 2)
            corner[k] = cor_r[p, k].astype(F32)
            for h in range(2):
                for q in range(3):
                    m = 4 * (src0 + q)
                    pad[h, base + q, first : first + 4, :] = corner[k, m : m + 4, h * 128 : (h + 1) * 128]
        for h in range(2):
            lanes = slice(h * 128, (h + 1) * 128)
            pad[h, base : base + 3, LEFT : LEFT + W, :] = row_r[p, 0 if top else 1, :, :, lanes].astype(F32)

    for row0 in ORDER:
        halo_start(0, saved, row0)
    for load in loads[1:]:
        load.wait()
    for n in range(HID // 256):
        units = slice(n * 256, (n + 1) * 256)
        wo_t[:, units] = w_out[units, :].T
        wi_t[units, :] = w_in[:, units].T
    for row0 in ORDER:
        halo_wait(0, row0)
        unpack(xpad, 0, row0)

    @pl.loop(0, H // CONV_ROWS)
    def _(n):
        conv = conv_rows(xpad, taps, n * CONV_ROWS, False) + cbias[...]
        pix = pl.ds(pl.multiple_of(n * (CONV_ROWS * W), CONV_ROWS * W), CONV_ROWS * W)
        centred = conv - jnp.mean(conv, axis=-1, keepdims=True)
        inv_std = lax.rsqrt(jnp.mean(centred * centred, axis=-1, keepdims=True) + EPS)
        standard = centred * inv_std
        std[pix, :] = standard
        inv[pix, :] = jnp.broadcast_to(inv_std, (CONV_ROWS * W, 128))
        nbuf[pix, :] = (standard * gain[...] + nbias[...]).astype(BF16)

    @pl.loop(0, HID // 256)
    def _(n):
        units = pl.ds(pl.multiple_of(n * 256, 256), 256)
        pre = jnp.dot(nbuf[...], w_in[:, units], preferred_element_type=F32) + b_in[:, units]
        square = pre * pre
        th = jnp.tanh(GELU_A * (pre + GELU_B * (square * pre)))
        half = 0.5 * (1.0 + th)
        hbuf[:, units] = (pre * half).astype(BF16)
        slope = GELU_A * (1.0 + (3.0 * GELU_B) * square)
        dgelu[:, units] = half + 0.5 * pre * (1.0 - th * th) * slope

    def shift_copy(src, n):
        rows = pl.ds(ORDER[n], CONV_ROWS)
        return pltpu.make_async_remote_copy(
            src_ref=src.at[rows],
            dst_ref=gin.at[rows],
            send_sem=shift_send.at[n],
            recv_sem=shift_recv.at[n],
            device_id=(lax.rem(seg + SEGS - 1, SEGS), r, c),
            device_id_type=MESH,
        )

    mask = tissue[...].astype(F32)

    def turn():
        tbuf[...] = nbuf[...].T
        for n in range(HID // 256):
            htbuf[n * 256 : (n + 1) * 256, :] = hbuf[:, n * 256 : (n + 1) * 256].T

    @pl.when(seg == SEGS - 1)
    def _():
        gin[...] = og[...]

    @pl.when(seg < SEGS - 1)
    def _():
        turn()

    for n, row0 in enumerate(ORDER):

        @pl.when(seg < SEGS - 1)
        def _(n=n):
            shift_copy(out, n).wait_recv()

        rows = slice(row0, row0 + CONV_ROWS)
        pix = slice(row0 * W, row0 * W + CH_PIX)
        upstream = gin[rows].reshape(CH_PIX, C).astype(F32)
        bg = (mask * lscale[...] * upstream).astype(BF16)
        bgb[pix, :] = bg
        hidden_grad = jnp.dot(bg, wo_t[...], preferred_element_type=F32)
        pg = (hidden_grad * dgelu[pix, :]).astype(BF16)
        pgb[pix, :] = pg
        ng = jnp.dot(pg, wi_t[...], preferred_element_type=F32) * gain[...]
        standard = std[pix, :]
        m1 = jnp.mean(ng, axis=-1, keepdims=True)
        m2 = jnp.mean(ng * standard, axis=-1, keepdims=True)
        cg = (inv[pix, 0:1] * (ng - m1 - standard * m2)).astype(BF16)
        cgt[rows] = cg.reshape(CONV_ROWS, W, C)
        wide = cg.astype(F32).reshape(CONV_ROWS, W, C)
        for h in range(2):
            gpad[h, 3 + row0 : 3 + row0 + CONV_ROWS, LEFT : LEFT + W, :] = wide[:, :, h * 128 : (h + 1) * 128]
        stage_cols(gpad, 1, row0)
        halo_start(1, cgt, row0)

    def remote(src, dst, send, recv, device):
        return pltpu.make_async_remote_copy(
            src_ref=src, dst_ref=dst, send_sem=send, recv_sem=recv,
            device_id=device, device_id_type=MESH,
        )

    def all_of(ref, send, recv):
        return remote(ref, ref, send, recv, sib)

    def sib_copy(src, dst, k):
        return remote(src, dst, sib_send.at[k], sib_recv.at[k], sib)

    other = 1 - core
    first_i = sib_copy(s0i.at[other], r0i, 0)
    first_o = sib_copy(s0o.at[other], r0o, 1)
    tap_a = sib_copy(ts0.at[other], tr0, 2)

    def gradients():
        for n in range(HID // 256):
            units = slice(n * 256, (n + 1) * 256)
            gi = jnp.dot(tbuf[...], pgb[:, units], preferred_element_type=F32) * scale
            gi = gi.astype(BF16)
            for k in range(COLS):
                s0i[k % 2, k // 2, :, units] = gi[16 * k : 16 * k + 16]
        first_i.start()
        for n in range(HID // 256):
            go = jnp.dot(htbuf[n * 256 : (n + 1) * 256, :], bgb[...], preferred_element_type=F32) * scale
            go = go.astype(BF16)
            for k in range(4):
                owner = n * 4 + k
                s0o[owner % 2, owner // 2] = go[64 * k : 64 * k + 64]
        first_o.start()
        for h in range(2):
            for j in range(7):
                sums = [jnp.zeros((8, 128), F32) for _ in range(7)]
                for block in range(H // CONV_ROWS):
                    row0 = block * CONV_ROWS
                    window = xpad[h, row0 : row0 + CONV_ROWS + 6, LEFT - 3 + j : LEFT - 3 + j + W, :]
                    grad = gpad[h, 3 + row0 : 3 + row0 + CONV_ROWS, LEFT : LEFT + W, :]
                    for i in range(7):
                        prod = (window[i : i + CONV_ROWS] * grad).reshape(2 * CONV_ROWS, 8, 128)
                        sums[i] = sums[i] + jnp.sum(prod, axis=0)
                for i in range(7):
                    tacc[h, 7 * i + j] = sums[i]
        for h in range(2):
            ts0[h] = jnp.zeros((64, 128), BF16)
            ts0[h, 0:49] = (jnp.sum(tacc[h], axis=1) * scale).astype(BF16)
        tap_a.start()

    near = jnp.where(core == 0, y, r)
    away = jnp.where(core == 0, r, y)

    def side_peer(k, along_y):
        return (seg, jnp.where(along_y, r, zpeer(k)), jnp.where(along_y, 2 * ypeer(k) + core, c))

    def a_copy(k):
        p = ypeer(k)
        return remote(t1i.at[p], r1i.at[k - 1], a_send, a_recv, (seg, r, 2 * p + core))

    def b_copy(k):
        p = zpeer(k)
        return remote(t1o.at[p], r1o.at[k - 1], b_send, b_recv, (seg, p, c))

    def ty_copy(k):
        return remote(try_.at[near], try_.at[near], ty_send, ty_recv, side_peer(k, core == 0))

    def input_gradient():
        for n, row0 in enumerate(ORDER):
            for needed in ((0, 4), (12, 8))[n] if n < 2 else ():
                halo_wait(1, needed)
                unpack(gpad, 1, needed)
            total = conv_rows(gpad, taps, row0, True).reshape(CONV_ROWS, W, C)
            total = gin[row0 : row0 + CONV_ROWS].astype(F32) + total
            out[row0 : row0 + CONV_ROWS] = total.astype(BF16)

            @pl.when(seg > 0)
            def _(n=n):
                shift_copy(out, n).start()

    def first_stage():
        first_i.wait()
        for k in range(YS):
            t1i[k] = (s0i[core, k].astype(F32) + r0i[k].astype(F32)).astype(BF16)

        for k in FAR:
            a_copy(k).start()
        first_o.wait()
        for k in range(YS):
            both = s0o[core, k].astype(F32) + r0o[k].astype(F32)
            both = both.astype(BF16)
            for q in range(ROWS):
                t1o[q, k] = both[16 * (q // 2) : 16 * (q // 2) + 16, 128 * (q % 2) : 128 * (q % 2) + 128]

        for k in FAR:
            b_copy(k).start()

        tap_a.wait()
        try_[near] = (ts0[core].astype(F32) + tr0[...].astype(F32)).astype(BF16)

        for k in FAR:
            ty_copy(k).start()

    @pl.when(seg == 0)
    def _():
        gradients()
        first_stage()
        input_gradient()

    @pl.when(seg == SEGS - 1)
    def _():
        input_gradient()
        turn()

    @pl.when(jnp.logical_and(seg > 0, seg < SEGS - 1))
    def _():
        input_gradient()

    @pl.when(seg > 0)
    def _():
        gradients()
        first_stage()

    all_of(r1i, a_send, a_recv).wait_recv()
    mine = t1i[y].astype(F32)
    for k in range(7):
        mine = mine + r1i[k].astype(F32)
    mine = mine.astype(BF16)
    for q in range(ROWS):
        p2i[q] = mine[:, 128 * q : 128 * q + 128]

    def c_copy(k):
        p = zpeer(k)
        return remote(p2i.at[p], r2i.at[k - 1], c_send, c_recv, (seg, p, c))

    for k in FAR:
        c_copy(k).start()

    all_of(r1o, b_send, b_recv).wait_recv()
    part = t1o[r].astype(F32)
    for k in range(7):
        part = part + r1o[k].astype(F32)
    p2o[...] = part.astype(BF16)

    def d_copy(k):
        p = ypeer(k)
        return remote(p2o.at[p], r2o.at[k - 1], d_send, d_recv, (seg, r, 2 * p + core))

    for k in FAR:
        d_copy(k).start()

    all_of(try_.at[pl.ds(0, 7)], ty_send, ty_recv).wait_recv()
    tsum = try_[0].astype(F32)
    for k in range(1, 8):
        tsum = tsum + try_[k].astype(F32)
    trz[away] = tsum.astype(BF16)

    def tz_copy(k):
        return remote(trz.at[away], trz.at[away], tz_send, tz_recv, side_peer(k, core == 1))

    for k in FAR:
        tz_copy(k).start()

    all_of(r2i, c_send, c_recv).wait_recv()
    full_i = p2i[r].astype(F32)
    for k in range(7):
        full_i = full_i + r2i[k].astype(F32)
    all_of(r2o, d_send, d_recv).wait_recv()
    full_o = p2o[y].astype(F32)
    for k in range(7):
        full_o = full_o + r2o[k].astype(F32)
    r3[r, 0] = full_i.astype(BF16)
    r3[r, 1] = full_o.astype(BF16)

    def e_copy(k):
        return remote(r3.at[r], r3.at[r], e_send, e_recv, (seg, zpeer(k), c))

    for k in FAR:
        e_copy(k).start()

    all_of(trz.at[pl.ds(0, 7)], tz_send, tz_recv).wait_recv()
    tsum = trz[0].astype(F32)
    for k in range(1, 8):
        tsum = tsum + trz[k].astype(F32)
    tfin[core] = tsum
    tap_b = sib_copy(tfin.at[core], tfin.at[core], 3)
    tap_b.start()

    all_of(r3.at[pl.ds(0, 7)], e_send, e_recv).wait_recv()
    for q in range(ROWS):
        gi_out[:, 128 * q : 128 * q + 128] = r3[q, 0].astype(F32)
        go_out[16 * (q // 2) : 16 * (q // 2) + 16, 128 * (q % 2) : 128 * (q % 2) + 128] = r3[q, 1].astype(F32)

    tap_b.wait_send()
    sib_copy(tfin.at[other], tfin.at[other], 3).wait_recv()
    for h in range(2):
        for i in range(7):
            taps_out[i, :, 0, h * 128 : (h + 1) * 128] = tfin[h, 7 * i : 7 * i + 7, :]

    halo_drain(0, saved)
    halo_drain(1, cgt)
    for n in range(CHUNKS):

        @pl.when(seg > 0)
        def _(n=n):
            shift_copy(out, n).wait_send()

    for ref, send, recv in (
        (r1i, a_send, a_recv),
        (r1o, b_send, b_recv),
        (r2i, c_send, c_recv),
        (r2o, d_send, d_recv),
        (r3.at[pl.ds(0, 7)], e_send, e_recv),
        (try_.at[pl.ds(0, 7)], ty_send, ty_recv),
        (trz.at[pl.ds(0, 7)], tz_send, tz_recv),
    ):
        all_of(ref, send, recv).wait_send()


def place(a, b, c, d, a_out, b_out, c_out, d_out, sem):
    pairs = zip((a, b, c, d), (a_out, b_out, c_out, d_out))
    copies = [pltpu.make_async_copy(x, z, sem.at[n]) for n, (x, z) in enumerate(pairs)]
    for copy in copies:
        copy.start()
    for copy in copies:
        copy.wait()


def per_device(
    saved_inputs, out_grad, tissue, conv_taps, conv_bias, norm_gain, norm_bias,
    w_in, b_in, w_out, layer_scale,
):
    scale = 1.0 / math.sqrt(ROWS * H * COLS * W)
    vmem = pl.BlockSpec(memory_space=pltpu.VMEM)
    dma = pltpu.SemaphoreType.DMA
    px = H * W
    out, gi, go, gt = pl.pallas_call(
        functools.partial(body, scale),
        out_shape=(
            pltpu.VMEM((H, W, C), BF16),
            pltpu.VMEM((C // COLS, HID), F32),
            pltpu.VMEM((HID // COLS, C), F32),
            pltpu.VMEM((7, 7, 1, C), F32),
        ),
        in_specs=[pl.BlockSpec(memory_space=pl.ANY)] * 11,
        out_specs=(vmem, vmem, vmem, vmem),
        scratch_shapes=[
            pltpu.VMEM((H, W, C), BF16),
            pltpu.VMEM((H, W, C), BF16),
            pltpu.VMEM((1, 1), jnp.int32),
            pltpu.VMEM((7, 7, 1, C), F32),
            pltpu.VMEM((1, C), F32),
            pltpu.VMEM((1, C), F32),
            pltpu.VMEM((1, C), F32),
            pltpu.VMEM((C, HID), BF16),
            pltpu.VMEM((1, HID), F32),
            pltpu.VMEM((HID, C), BF16),
            pltpu.VMEM((1, C), F32),
            dma((11,)),
            pltpu.VMEM((C, px), BF16),
            pltpu.VMEM((HID, px), BF16),
            pltpu.VMEM((C, HID), BF16),
            pltpu.VMEM((HID, C), BF16),
            pltpu.VMEM((2, H + 6, PADW, 128), F32),
            pltpu.VMEM((2, H + 6, PADW, 128), F32),
            pltpu.VMEM((px, C), F32),
            pltpu.VMEM((px, 128), F32),
            pltpu.VMEM((px, C), BF16),
            pltpu.VMEM((px, HID), BF16),
            pltpu.VMEM((px, HID), F32),
            pltpu.VMEM((px, C), BF16),
            pltpu.VMEM((px, HID), BF16),
            pltpu.VMEM((H, W, C), BF16),
            pltpu.VMEM((H, W, C), BF16),
            pltpu.VMEM((2, 2, 4 * H, C), BF16),
            pltpu.VMEM((2, 2, 3, W, C), BF16),
            pltpu.VMEM((2, 2, 4 * H, C), BF16),
            pltpu.VMEM((2, 4, 16, C), BF16),
            pltpu.VMEM((2, 4 * H, C), F32),
            pltpu.VMEM((4, 16, C), F32),
            pltpu.VMEM((2, YS, 16, HID), BF16),
            pltpu.VMEM((2, YS, 64, C), BF16),
            pltpu.VMEM((YS, 16, HID), BF16),
            pltpu.VMEM((YS, 64, C), BF16),
            pltpu.VMEM((YS, 16, HID), BF16),
            pltpu.VMEM((ROWS, YS, 16, 128), BF16),
            pltpu.VMEM((7, 16, HID), BF16),
            pltpu.VMEM((7, YS, 16, 128), BF16),
            pltpu.VMEM((ROWS, 16, 128), BF16),
            pltpu.VMEM((YS, 16, 128), BF16),
            pltpu.VMEM((7, 16, 128), BF16),
            pltpu.VMEM((7, 16, 128), BF16),
            pltpu.VMEM((ROWS, 2, 16, 128), BF16),
            pltpu.VMEM((2, 49, 8, 128), F32),
            pltpu.VMEM((2, 64, 128), BF16),
            pltpu.VMEM((64, 128), BF16),
            pltpu.VMEM((YS, 64, 128), BF16),
            pltpu.VMEM((ROWS, 64, 128), BF16),
            pltpu.VMEM((2, 64, 128), F32),
            dma((2, 16)), dma((2, 16)), dma((CHUNKS,)), dma((CHUNKS,)),
            dma((4,)), dma((4,)),
            dma, dma, dma, dma, dma, dma, dma, dma,
            dma, dma, dma, dma, dma, dma,
        ],
        compiler_params=pltpu.CompilerParams(collective_id=0, has_side_effects=True),
    )(*(operand for operand in (
        saved_inputs[0, 0], out_grad[0], tissue[0], conv_taps.reshape(7, 7, 1, C), conv_bias, norm_gain, norm_bias,
        w_in[0], b_in, w_out[0], layer_scale,
    )))
    results = (out, gi, go, gt)
    hbm = pl.BlockSpec(memory_space=pl.ANY)
    out, gi, go, gt = pl.pallas_call(
        place,
        out_shape=tuple(jax.ShapeDtypeStruct(a.shape, a.dtype) for a in results),
        in_specs=[vmem] * 4,
        out_specs=(hbm, hbm, hbm, hbm),
        scratch_shapes=[dma((4,))],
        compiler_params=pltpu.CompilerParams(vmem_limit_bytes=4 * 1024 * 1024),
    )(*results)
    return (out[None, None], gi[None], go[None], gt.reshape(1, 7, 7, C))


def solution(mesh):
    return jax.shard_map(
        per_device,
        mesh=mesh,
        in_specs=(
            P("segment", None, "row", "col", None),
            P(None, "row", "col", None),
            P(None, "row", "col"),
            P("segment", None, None, None),
            P("segment", None),
            P("segment", None),
            P("segment", None),
            P("segment", None, None),
            P("segment", None),
            P("segment", None, None),
            P("segment", None),
        ),
        out_specs=(
            P("segment", None, "row", "col", None),
            P("segment", "col", None),
            P("segment", "col", None),
            P("segment", None, None, None),
        ),
        check_vma=False,
    )
```

```python
import functools
import math

import jax
import jax.numpy as jnp
from jax import lax
from jax.experimental import pallas as pl
from jax.experimental.pallas import tpu as pltpu
from jax.sharding import PartitionSpec as P

F32 = jnp.float32
BF16 = jnp.bfloat16
MESH = pl.DeviceIdType.MESH
EPS = 1e-06
VMEM_MAIN = 28 * 1024 * 1024
H = 16
W = 16
C = 256
HID = 1024
ROWS = 8
COLS = 16
YS = 8
SEGS = 4
LEFT = 8
PADW = 32
CONV_ROWS = 4
ORDER = (0, 12, 4, 8)
CHUNKS = len(ORDER)
CH_PIX = CONV_ROWS * W
DIRS = ((-1, 0), (1, 0), (0, -1), (0, 1), (-1, -1), (-1, 1), (1, -1), (1, 1))
BACK = (1, 0, 3, 2, 7, 6, 5, 4)
FAR = (4, 3, 5, 2, 6, 1, 7)
GELU_A = math.sqrt(2.0 / math.pi)
GELU_B = 0.044715


def conv_rows(pad, taps, row0, flip):
    halves = []
    for h in range(2):
        acc = jnp.zeros((CONV_ROWS, W, 128), F32)
        for j in range(7):
            window = pad[h, pl.ds(row0, CONV_ROWS + 6), LEFT - 3 + j : LEFT - 3 + j + W, :]
            for i in range(7):
                ti, tj = (6 - i, 6 - j) if flip else (i, j)
                tap = taps[ti, tj, :, h * 128 : (h + 1) * 128]
                acc = acc + tap[None] * window[i : i + CONV_ROWS]
        halves.append(acc.reshape(CONV_ROWS * W, 128))
    return jnp.concatenate(halves, axis=-1)


def body(
    scale,
    saved_h, og_h, tissue_h, taps_h, cbias_h, gain_h, nbias_h, w_in_h, b_in_h, w_out_h, lscale_h,
    out, gi_out, go_out, taps_out,
    saved, og, tissue, taps, cbias, gain, nbias, w_in, b_in, w_out, lscale, load_sem, tbuf, htbuf, wo_t, wi_t,
    xpad, gpad, std, inv, nbuf, hbuf, dgelu, bgb, pgb, gin, cgt,
    col_s, row_r, col_r, cor_r, strip, corner,
    s0i, s0o, r0i, r0o, t1i, t1o, r1i, r1o, p2i, p2o, r2i, r2o, r3,
    tacc, ts0, tr0, try_, trz, tfin,
    halo_send, halo_recv, shift_send, shift_recv,
    sib_send, sib_recv, a_send, a_recv, b_send, b_recv,
    c_send, c_recv, d_send, d_recv, e_send, e_recv, ty_send, ty_recv, tz_send, tz_recv,
):
    seg = lax.axis_index("segment")
    r = lax.axis_index("row")
    c = lax.axis_index("col")
    core = lax.rem(c, 2)
    y = lax.div(c, 2)
    sib = (seg, r, c + 1 - 2 * core)
    off_c = c + 2 * core - 1
    off_ok = jnp.logical_and(off_c >= 0, off_c < COLS)

    def near_ok(d):
        dr, dc = DIRS[d]
        ok = None
        if dr:
            ok = (r > 0) if dr < 0 else (r < ROWS - 1)
        if dc:
            okc = (c > 0) if dc < 0 else (c < COLS - 1)
            ok = okc if ok is None else jnp.logical_and(ok, okc)
        return ok

    def near_id(d):
        dr, dc = DIRS[d]
        return (seg, r + dr, c + dc)

    def zpeer(k):
        return lax.rem(r + k, ROWS)

    def ypeer(k):
        return lax.rem(y + k, YS)

    sources = (saved_h, taps_h, cbias_h, gain_h, nbias_h, w_in_h, b_in_h, w_out_h, lscale_h, tissue_h, og_h)
    places = (saved, taps, cbias, gain, nbias, w_in, b_in, w_out, lscale, tissue, og)
    loads = [pltpu.make_async_copy(a, b, load_sem.at[n]) for n, (a, b) in enumerate(zip(sources, places))]
    for load in loads:
        load.start()

    barrier = pltpu.get_barrier_semaphore()

    def greet(device):
        pl.semaphore_signal(barrier, inc=1, device_id=device, device_id_type=MESH)

    greet(sib)
    count = 1 + 2 * 7
    for k in range(1, 8):
        greet((seg, zpeer(k), c))
        greet((seg, r, 2 * ypeer(k) + core))

    @pl.when(off_ok)
    def _():
        greet((seg, r, off_c))

    count = count + jnp.where(off_ok, 1, 0)
    for d in range(4, 8):
        ok = near_ok(d)

        @pl.when(ok)
        def _(d=d):
            greet(near_id(d))

        count = count + jnp.where(ok, 1, 0)

    @pl.when(seg > 0)
    def _():
        greet((seg - 1, r, c))

    @pl.when(seg < SEGS - 1)
    def _():
        greet((seg + 1, r, c))

    count = count + jnp.where(seg > 0, 1, 0) + jnp.where(seg < SEGS - 1, 1, 0)

    def stage_cols(pad, p, row0):
        piece = slice(4 * row0, 4 * row0 + 16)
        for side, first in ((0, LEFT), (1, LEFT + W - 4)):
            for h in range(2):
                for q in range(row0, row0 + CONV_ROWS):
                    strip[side, 4 * q : 4 * q + 4, h * 128 : (h + 1) * 128] = pad[h, 3 + q, first : first + 4, :]
            col_s[p, side, piece] = strip[side, piece].astype(BF16)

    loads[0].wait()
    for h in range(2):
        xpad[h, 3 : 3 + H, LEFT : LEFT + W, :] = saved[:, :, h * 128 : (h + 1) * 128].astype(F32)
    for row0 in ORDER:
        stage_cols(xpad, 0, row0)

    def landing(p, d, m=0):
        if d < 2:
            return row_r.at[p, d]
        if d < 4:
            return col_r.at[p, d - 2, pl.ds(16 * m, 16)]
        return cor_r.at[p, d - 4]

    def slot(d, m=0):
        return d if d not in (2, 3) else 8 + 4 * (d - 2) + m

    for p in range(2):
        for d in range(8):

            @pl.when(jnp.logical_not(near_ok(d)))
            def _(p=p, d=d):
                for m in range(4 if d in (2, 3) else 1):
                    ref = landing(p, d, m)
                    ref[...] = jnp.zeros(ref.shape, BF16)

    pl.semaphore_wait(barrier, count)

    def halo_copy(p, tile, d, m=0):
        dr, dc = DIRS[d]
        side = 0 if dc < 0 else 1
        if dc == 0:
            src = tile.at[0:3] if dr < 0 else tile.at[H - 3 : H]
        elif dr == 0:
            src = col_s.at[p, side, pl.ds(16 * m, 16)]
        else:
            src = col_s.at[p, side, pl.ds(0 if dr < 0 else 4 * H - 16, 16)]
        return pltpu.make_async_remote_copy(
            src_ref=src,
            dst_ref=landing(p, BACK[d], m),
            send_sem=halo_send.at[p, slot(d, m)],
            recv_sem=halo_recv.at[p, slot(BACK[d], m)],
            device_id=near_id(d),
            device_id_type=MESH,
        )

    def messages(row0):
        m = row0 // CONV_ROWS
        edge = ((4, 0), (5, 0), (0, 0)) if row0 == 0 else ((6, 0), (7, 0), (1, 0)) if row0 == H - CONV_ROWS else ()
        return edge + ((2, m), (3, m))

    def halo_start(p, tile, row0):
        for d, m in messages(row0):

            @pl.when(near_ok(d))
            def _(d=d, m=m):
                halo_copy(p, tile, d, m).start()

    def halo_wait(p, row0):
        for d, m in messages(row0):

            @pl.when(near_ok(d))
            def _(d=d, m=m):
                pltpu.make_async_remote_copy(
                    src_ref=landing(p, d, m),
                    dst_ref=landing(p, d, m),
                    send_sem=halo_send.at[p, slot(d, m)],
                    recv_sem=halo_recv.at[p, slot(d, m)],
                    device_id=near_id(d),
                    device_id_type=MESH,
                ).wait_recv()

    def halo_drain(p, tile):
        for row0 in ORDER:
            for d, m in messages(row0):

                @pl.when(near_ok(d))
                def _(d=d, m=m):
                    halo_copy(p, tile, d, m).wait_send()

    def unpack(pad, p, row0):
        piece = slice(4 * row0, 4 * row0 + 16)
        for side, first in ((0, LEFT - 4), (1, LEFT + W)):
            strip[side, piece] = col_r[p, side, piece].astype(F32)
            for h in range(2):
                for q in range(row0, row0 + CONV_ROWS):
                    pad[h, 3 + q, first : first + 4, :] = strip[side, 4 * q : 4 * q + 4, h * 128 : (h + 1) * 128]
        if row0 not in (0, H - CONV_ROWS):
            return
        top = row0 == 0
        base, src0 = (0, 1) if top else (3 + H, 0)
        for side, first in ((0, LEFT - 4), (1, LEFT + W)):
            k = side + (0 if top else 2)
            corner[k] = cor_r[p, k].astype(F32)
            for h in range(2):
                for q in range(3):
                    m = 4 * (src0 + q)
                    pad[h, base + q, first : first + 4, :] = corner[k, m : m + 4, h * 128 : (h + 1) * 128]
        for h in range(2):
            lanes = slice(h * 128, (h + 1) * 128)
            pad[h, base : base + 3, LEFT : LEFT + W, :] = row_r[p, 0 if top else 1, :, :, lanes].astype(F32)

    for row0 in ORDER:
        halo_start(0, saved, row0)
    for load in loads[1:]:
        load.wait()
    for n in range(HID // 256):
        units = slice(n * 256, (n + 1) * 256)
        wo_t[:, units] = w_out[units, :].T
        wi_t[units, :] = w_in[:, units].T
    for row0 in ORDER:
        halo_wait(0, row0)
        unpack(xpad, 0, row0)

    for row0 in range(0, H, CONV_ROWS):
        conv = conv_rows(xpad, taps, row0, False) + cbias[...]
        pix = slice(row0 * W, (row0 + CONV_ROWS) * W)
        centred = conv - jnp.mean(conv, axis=-1, keepdims=True)
        inv_std = lax.rsqrt(jnp.mean(centred * centred, axis=-1, keepdims=True) + EPS)
        standard = centred * inv_std
        std[pix, :] = standard
        inv[pix, :] = jnp.broadcast_to(inv_std, (CONV_ROWS * W, 128))
        nbuf[pix, :] = (standard * gain[...] + nbias[...]).astype(BF16)

    @pl.loop(0, HID // 256)
    def _(n):
        units = pl.ds(pl.multiple_of(n * 256, 256), 256)
        pre = jnp.dot(nbuf[...], w_in[:, units], preferred_element_type=F32) + b_in[:, units]
        square = pre * pre
        th = jnp.tanh(GELU_A * (pre + GELU_B * (square * pre)))
        half = 0.5 * (1.0 + th)
        hbuf[:, units] = (pre * half).astype(BF16)
        slope = GELU_A * (1.0 + (3.0 * GELU_B) * square)
        dgelu[:, units] = half + 0.5 * pre * (1.0 - th * th) * slope

    def shift_copy(src, n):
        rows = pl.ds(ORDER[n], CONV_ROWS)
        return pltpu.make_async_remote_copy(
            src_ref=src.at[rows],
            dst_ref=gin.at[rows],
            send_sem=shift_send.at[n],
            recv_sem=shift_recv.at[n],
            device_id=(lax.rem(seg + SEGS - 1, SEGS), r, c),
            device_id_type=MESH,
        )

    mask = tissue[...].astype(F32)

    def turn():
        tbuf[...] = nbuf[...].T
        for n in range(HID // 256):
            htbuf[n * 256 : (n + 1) * 256, :] = hbuf[:, n * 256 : (n + 1) * 256].T

    @pl.when(seg == SEGS - 1)
    def _():
        gin[...] = og[...]

    @pl.when(seg < SEGS - 1)
    def _():
        turn()

    for n, row0 in enumerate(ORDER):

        @pl.when(seg < SEGS - 1)
        def _(n=n):
            shift_copy(out, n).wait_recv()

        rows = slice(row0, row0 + CONV_ROWS)
        pix = slice(row0 * W, row0 * W + CH_PIX)
        upstream = gin[rows].reshape(CH_PIX, C).astype(F32)
        bg = (mask * lscale[...] * upstream).astype(BF16)
        bgb[pix, :] = bg
        hidden_grad = jnp.dot(bg, wo_t[...], preferred_element_type=F32)
        pg = (hidden_grad * dgelu[pix, :]).astype(BF16)
        pgb[pix, :] = pg
        ng = jnp.dot(pg, wi_t[...], preferred_element_type=F32) * gain[...]
        standard = std[pix, :]
        m1 = jnp.mean(ng, axis=-1, keepdims=True)
        m2 = jnp.mean(ng * standard, axis=-1, keepdims=True)
        cg = (inv[pix, 0:1] * (ng - m1 - standard * m2)).astype(BF16)
        cgt[rows] = cg.reshape(CONV_ROWS, W, C)
        wide = cg.astype(F32).reshape(CONV_ROWS, W, C)
        for h in range(2):
            gpad[h, 3 + row0 : 3 + row0 + CONV_ROWS, LEFT : LEFT + W, :] = wide[:, :, h * 128 : (h + 1) * 128]
        stage_cols(gpad, 1, row0)
        halo_start(1, cgt, row0)

    def remote(src, dst, send, recv, device):
        return pltpu.make_async_remote_copy(
            src_ref=src, dst_ref=dst, send_sem=send, recv_sem=recv,
            device_id=device, device_id_type=MESH,
        )

    def all_of(ref, send, recv):
        return remote(ref, ref, send, recv, sib)

    def sib_copy(src, dst, k):
        return remote(src, dst, sib_send.at[k], sib_recv.at[k], sib)

    other = 1 - core
    first_i = sib_copy(s0i.at[other], r0i, 0)
    first_o = sib_copy(s0o.at[other], r0o, 1)
    tap_a = sib_copy(ts0.at[other], tr0, 2)

    def gradients():
        for n in range(HID // 256):
            units = slice(n * 256, (n + 1) * 256)
            gi = jnp.dot(tbuf[...], pgb[:, units], preferred_element_type=F32) * scale
            gi = gi.astype(BF16)
            for k in range(COLS):
                s0i[k % 2, k // 2, :, units] = gi[16 * k : 16 * k + 16]
        first_i.start()
        for n in range(HID // 256):
            go = jnp.dot(htbuf[n * 256 : (n + 1) * 256, :], bgb[...], preferred_element_type=F32) * scale
            go = go.astype(BF16)
            for k in range(4):
                owner = n * 4 + k
                s0o[owner % 2, owner // 2] = go[64 * k : 64 * k + 64]
        first_o.start()
        for h in range(2):
            for j in range(7):
                sums = [jnp.zeros((8, 128), F32) for _ in range(7)]
                for block in range(H // CONV_ROWS):
                    row0 = block * CONV_ROWS
                    window = xpad[h, row0 : row0 + CONV_ROWS + 6, LEFT - 3 + j : LEFT - 3 + j + W, :]
                    grad = gpad[h, 3 + row0 : 3 + row0 + CONV_ROWS, LEFT : LEFT + W, :]
                    for i in range(7):
                        prod = (window[i : i + CONV_ROWS] * grad).reshape(2 * CONV_ROWS, 8, 128)
                        sums[i] = sums[i] + jnp.sum(prod, axis=0)
                for i in range(7):
                    tacc[h, 7 * i + j] = sums[i]
        for h in range(2):
            ts0[h] = jnp.zeros((64, 128), BF16)
            ts0[h, 0:49] = (jnp.sum(tacc[h], axis=1) * scale).astype(BF16)
        tap_a.start()

    near = jnp.where(core == 0, y, r)
    away = jnp.where(core == 0, r, y)

    def side_peer(k, along_y):
        return (seg, jnp.where(along_y, r, zpeer(k)), jnp.where(along_y, 2 * ypeer(k) + core, c))

    def a_copy(k):
        p = ypeer(k)
        return remote(t1i.at[p], r1i.at[k - 1], a_send, a_recv, (seg, r, 2 * p + core))

    def b_copy(k):
        p = zpeer(k)
        return remote(t1o.at[p], r1o.at[k - 1], b_send, b_recv, (seg, p, c))

    def ty_copy(k):
        return remote(try_.at[near], try_.at[near], ty_send, ty_recv, side_peer(k, core == 0))

    def input_gradient():
        for n, row0 in enumerate(ORDER):
            for needed in ((0, 4), (12, 8))[n] if n < 2 else ():
                halo_wait(1, needed)
                unpack(gpad, 1, needed)
            total = conv_rows(gpad, taps, row0, True).reshape(CONV_ROWS, W, C)
            total = gin[row0 : row0 + CONV_ROWS].astype(F32) + total
            out[row0 : row0 + CONV_ROWS] = total.astype(BF16)

            @pl.when(seg > 0)
            def _(n=n):
                shift_copy(out, n).start()

    def first_stage():
        first_i.wait()
        for k in range(YS):
            t1i[k] = (s0i[core, k].astype(F32) + r0i[k].astype(F32)).astype(BF16)

        for k in FAR:
            a_copy(k).start()
        first_o.wait()
        for k in range(YS):
            both = s0o[core, k].astype(F32) + r0o[k].astype(F32)
            both = both.astype(BF16)
            for q in range(ROWS):
                t1o[q, k] = both[16 * (q // 2) : 16 * (q // 2) + 16, 128 * (q % 2) : 128 * (q % 2) + 128]

        for k in FAR:
            b_copy(k).start()

        tap_a.wait()
        try_[near] = (ts0[core].astype(F32) + tr0[...].astype(F32)).astype(BF16)

        for k in FAR:
            ty_copy(k).start()

    @pl.when(seg == 0)
    def _():
        gradients()
        first_stage()
        input_gradient()

    @pl.when(seg == SEGS - 1)
    def _():
        input_gradient()
        turn()

    @pl.when(jnp.logical_and(seg > 0, seg < SEGS - 1))
    def _():
        input_gradient()

    @pl.when(seg > 0)
    def _():
        gradients()
        first_stage()

    all_of(r1i, a_send, a_recv).wait_recv()
    mine = t1i[y].astype(F32)
    for k in range(7):
        mine = mine + r1i[k].astype(F32)
    mine = mine.astype(BF16)
    for q in range(ROWS):
        p2i[q] = mine[:, 128 * q : 128 * q + 128]

    def c_copy(k):
        p = zpeer(k)
        return remote(p2i.at[p], r2i.at[k - 1], c_send, c_recv, (seg, p, c))

    for k in FAR:
        c_copy(k).start()

    all_of(r1o, b_send, b_recv).wait_recv()
    part = t1o[r].astype(F32)
    for k in range(7):
        part = part + r1o[k].astype(F32)
    p2o[...] = part.astype(BF16)

    def d_copy(k):
        p = ypeer(k)
        return remote(p2o.at[p], r2o.at[k - 1], d_send, d_recv, (seg, r, 2 * p + core))

    for k in FAR:
        d_copy(k).start()

    all_of(try_.at[pl.ds(0, 7)], ty_send, ty_recv).wait_recv()
    tsum = try_[0].astype(F32)
    for k in range(1, 8):
        tsum = tsum + try_[k].astype(F32)
    trz[away] = tsum.astype(BF16)

    def tz_copy(k):
        return remote(trz.at[away], trz.at[away], tz_send, tz_recv, side_peer(k, core == 1))

    for k in FAR:
        tz_copy(k).start()

    all_of(r2i, c_send, c_recv).wait_recv()
    full_i = p2i[r].astype(F32)
    for k in range(7):
        full_i = full_i + r2i[k].astype(F32)
    all_of(r2o, d_send, d_recv).wait_recv()
    full_o = p2o[y].astype(F32)
    for k in range(7):
        full_o = full_o + r2o[k].astype(F32)
    r3[r, 0] = full_i.astype(BF16)
    r3[r, 1] = full_o.astype(BF16)

    def e_copy(k):
        return remote(r3.at[r], r3.at[r], e_send, e_recv, (seg, zpeer(k), c))

    for k in FAR:
        e_copy(k).start()

    all_of(trz.at[pl.ds(0, 7)], tz_send, tz_recv).wait_recv()
    tsum = trz[0].astype(F32)
    for k in range(1, 8):
        tsum = tsum + trz[k].astype(F32)
    tfin[core] = tsum
    tap_b = sib_copy(tfin.at[core], tfin.at[core], 3)
    tap_b.start()

    all_of(r3.at[pl.ds(0, 7)], e_send, e_recv).wait_recv()
    for q in range(ROWS):
        gi_out[:, 128 * q : 128 * q + 128] = r3[q, 0].astype(F32)
        go_out[16 * (q // 2) : 16 * (q // 2) + 16, 128 * (q % 2) : 128 * (q % 2) + 128] = r3[q, 1].astype(F32)

    tap_b.wait_send()
    sib_copy(tfin.at[other], tfin.at[other], 3).wait_recv()
    for h in range(2):
        for i in range(7):
            taps_out[i, :, 0, h * 128 : (h + 1) * 128] = tfin[h, 7 * i : 7 * i + 7, :]

    halo_drain(0, saved)
    halo_drain(1, cgt)
    for n in range(CHUNKS):

        @pl.when(seg > 0)
        def _(n=n):
            shift_copy(out, n).wait_send()

    for ref, send, recv in (
        (r1i, a_send, a_recv),
        (r1o, b_send, b_recv),
        (r2i, c_send, c_recv),
        (r2o, d_send, d_recv),
        (r3.at[pl.ds(0, 7)], e_send, e_recv),
        (try_.at[pl.ds(0, 7)], ty_send, ty_recv),
        (trz.at[pl.ds(0, 7)], tz_send, tz_recv),
    ):
        all_of(ref, send, recv).wait_send()


def place(a, b, c, d, a_out, b_out, c_out, d_out, sem):
    pairs = zip((a, b, c, d), (a_out, b_out, c_out, d_out))
    copies = [pltpu.make_async_copy(x, z, sem.at[n]) for n, (x, z) in enumerate(pairs)]
    for copy in copies:
        copy.start()
    for copy in copies:
        copy.wait()


def per_device(
    saved_inputs, out_grad, tissue, conv_taps, conv_bias, norm_gain, norm_bias,
    w_in, b_in, w_out, layer_scale,
):
    scale = 1.0 / math.sqrt(ROWS * H * COLS * W)
    vmem = pl.BlockSpec(memory_space=pltpu.VMEM)
    dma = pltpu.SemaphoreType.DMA
    px = H * W
    out, gi, go, gt = pl.pallas_call(
        functools.partial(body, scale),
        out_shape=(
            pltpu.VMEM((H, W, C), BF16),
            pltpu.VMEM((C // COLS, HID), F32),
            pltpu.VMEM((HID // COLS, C), F32),
            pltpu.VMEM((7, 7, 1, C), F32),
        ),
        in_specs=[pl.BlockSpec(memory_space=pl.ANY)] * 11,
        out_specs=(vmem, vmem, vmem, vmem),
        scratch_shapes=[
            pltpu.VMEM((H, W, C), BF16),
            pltpu.VMEM((H, W, C), BF16),
            pltpu.VMEM((1, 1), jnp.int32),
            pltpu.VMEM((7, 7, 1, C), F32),
            pltpu.VMEM((1, C), F32),
            pltpu.VMEM((1, C), F32),
            pltpu.VMEM((1, C), F32),
            pltpu.VMEM((C, HID), BF16),
            pltpu.VMEM((1, HID), F32),
            pltpu.VMEM((HID, C), BF16),
            pltpu.VMEM((1, C), F32),
            dma((11,)),
            pltpu.VMEM((C, px), BF16),
            pltpu.VMEM((HID, px), BF16),
            pltpu.VMEM((C, HID), BF16),
            pltpu.VMEM((HID, C), BF16),
            pltpu.VMEM((2, H + 6, PADW, 128), F32),
            pltpu.VMEM((2, H + 6, PADW, 128), F32),
            pltpu.VMEM((px, C), F32),
            pltpu.VMEM((px, 128), F32),
            pltpu.VMEM((px, C), BF16),
            pltpu.VMEM((px, HID), BF16),
            pltpu.VMEM((px, HID), F32),
            pltpu.VMEM((px, C), BF16),
            pltpu.VMEM((px, HID), BF16),
            pltpu.VMEM((H, W, C), BF16),
            pltpu.VMEM((H, W, C), BF16),
            pltpu.VMEM((2, 2, 4 * H, C), BF16),
            pltpu.VMEM((2, 2, 3, W, C), BF16),
            pltpu.VMEM((2, 2, 4 * H, C), BF16),
            pltpu.VMEM((2, 4, 16, C), BF16),
            pltpu.VMEM((2, 4 * H, C), F32),
            pltpu.VMEM((4, 16, C), F32),
            pltpu.VMEM((2, YS, 16, HID), BF16),
            pltpu.VMEM((2, YS, 64, C), BF16),
            pltpu.VMEM((YS, 16, HID), BF16),
            pltpu.VMEM((YS, 64, C), BF16),
            pltpu.VMEM((YS, 16, HID), BF16),
            pltpu.VMEM((ROWS, YS, 16, 128), BF16),
            pltpu.VMEM((7, 16, HID), BF16),
            pltpu.VMEM((7, YS, 16, 128), BF16),
            pltpu.VMEM((ROWS, 16, 128), BF16),
            pltpu.VMEM((YS, 16, 128), BF16),
            pltpu.VMEM((7, 16, 128), BF16),
            pltpu.VMEM((7, 16, 128), BF16),
            pltpu.VMEM((ROWS, 2, 16, 128), BF16),
            pltpu.VMEM((2, 49, 8, 128), F32),
            pltpu.VMEM((2, 64, 128), BF16),
            pltpu.VMEM((64, 128), BF16),
            pltpu.VMEM((YS, 64, 128), BF16),
            pltpu.VMEM((ROWS, 64, 128), BF16),
            pltpu.VMEM((2, 64, 128), F32),
            dma((2, 16)), dma((2, 16)), dma((CHUNKS,)), dma((CHUNKS,)),
            dma((4,)), dma((4,)),
            dma, dma, dma, dma, dma, dma, dma, dma,
            dma, dma, dma, dma, dma, dma,
        ],
        compiler_params=pltpu.CompilerParams(collective_id=0, has_side_effects=True),
    )(*(operand for operand in (
        saved_inputs[0, 0], out_grad[0], tissue[0], conv_taps.reshape(7, 7, 1, C), conv_bias, norm_gain, norm_bias,
        w_in[0], b_in, w_out[0], layer_scale,
    )))
    results = (out, gi, go, gt)
    hbm = pl.BlockSpec(memory_space=pl.ANY)
    out, gi, go, gt = pl.pallas_call(
        place,
        out_shape=tuple(jax.ShapeDtypeStruct(a.shape, a.dtype) for a in results),
        in_specs=[vmem] * 4,
        out_specs=(hbm, hbm, hbm, hbm),
        scratch_shapes=[dma((4,))],
        compiler_params=pltpu.CompilerParams(vmem_limit_bytes=4 * 1024 * 1024),
    )(*results)
    return (out[None, None], gi[None], go[None], gt.reshape(1, 7, 7, C))


def solution(mesh):
    return jax.shard_map(
        per_device,
        mesh=mesh,
        in_specs=(
            P("segment", None, "row", "col", None),
            P(None, "row", "col", None),
            P(None, "row", "col"),
            P("segment", None, None, None),
            P("segment", None),
            P("segment", None),
            P("segment", None),
            P("segment", None, None),
            P("segment", None),
            P("segment", None, None),
            P("segment", None),
        ),
        out_specs=(
            P("segment", None, "row", "col", None),
            P("segment", "col", None),
            P("segment", "col", None),
            P("segment", None, None, None),
        ),
        check_vma=False,
    )
```
